256 devices in a mesh: segment: 16 (over y, z_hi), band: 16 (over z_lo, x, core).
Axes of the slice: x: 4, y: 4, z: 8 (z_hi: 4, z_lo: 2; z = z_hi * 2 + z_lo), core: 2. Of those that a mesh axis runs over, the one named last changes fastest.
Arguments:
- forward_state: bfloat16 [16, 2, 128, 64, 256], P('segment', None, 'band'), may hold values from -6 to 6
- returning_state: bfloat16 [16, 2, 128, 64, 256], P('segment', None, 'band'), may hold values from -6 to 6
- returning_grad: bfloat16 [16, 2, 128, 64, 256], P('segment', None, 'band'), may hold values from -6 to 6
- weights: bfloat16 [16, 2, 2304, 256], P('segment'), may hold values from -0.125 to 0.125
- fresh_input: bfloat16 [2, 2, 128, 64, 256], P(None, None, 'band'), may hold values from -6 to 6
- loss_grad: bfloat16 [2, 2, 128, 64, 256], P(None, None, 'band'), may hold values from -6 to 6
Outputs:
- forward_out: bfloat16 [16, 2, 128, 64, 256], P('segment', None, 'band')
- returning_out: bfloat16 [16, 2, 128, 64, 256], P('segment', None, 'band')
- backward_out: bfloat16 [16, 2, 128, 64, 256], P('segment', None, 'band')
- weight_grad: float32 [16, 2, 2304, 256], P('segment', None, 'band')
The draws below stay inside these ranges and needn't reach their ends.
All inputs are finite; a program needn't handle non-finite values.
Results may differ from the reference program's by a relative error of at most 0.02.
Values may be sent and summed in bfloat16 or wider, within the bound.
No kernel may reach another device: no remote copies, remote signals or barrier semaphores. Data moves between devices by JAX's collectives and lax.ppermute only.
A program may use at most 64 MiB of HBM per device.

```python
import jax
import jax.numpy as jnp
from jax import lax

CHANNELS = 256
TILE_COLS = 64
TICK_COUNT = 2
SEGMENTS = 16
HEIGHT = 128


def shard_levels(rng, shape, split, low, largest):
    def one(axis_at, shards_of):
        heights = jax.random.uniform(jax.random.fold_in(jax.random.fold_in(rng, 6), axis_at), (shards_of,), jnp.float32, low / len(split), largest / len(split))
        return jnp.repeat(jnp.exp(heights), shape[axis_at] // shards_of).reshape((-1,) + (1,) * (len(shape) - axis_at - 1))

    loudness = one(*split[0])
    for cut in split[1:]:
        loudness = loudness * one(*cut)
    return loudness


def noise(own_key, dims, deviation, most, shards=(), dtype=jnp.bfloat16):
    values = jax.random.normal(own_key, dims, jnp.float32) * deviation
    if len(shards) > 0:
        values = shard_levels(own_key, dims, shards, -0.22, 0.18) * values
    return jnp.clip(values, min=-most, max=most).astype(dtype)


def setup_inputs(seed: int = 0) -> dict:
    splits = jax.random.split(jax.random.key(seed), 7)
    return {
        "forward_state": noise(splits[0], (SEGMENTS, 2, HEIGHT, TILE_COLS, CHANNELS), 1.0, 6.0, ((0, 16), (2, 16))),
        "returning_state": noise(splits[1], (SEGMENTS, 2, HEIGHT, TILE_COLS, CHANNELS), 1.0, 6.0, ((0, 16), (2, 16))),
        "returning_grad": noise(splits[2], (SEGMENTS, 2, HEIGHT, TILE_COLS, CHANNELS), 1.0, 6.0, ((0, 16), (2, 16))),
        "weights": noise(splits[3], (SEGMENTS, 2, 9 * CHANNELS, CHANNELS), (9 * CHANNELS) ** -0.5, 0.125, ((0, 16),)),
        "fresh_input": noise(splits[4], (TICK_COUNT, 2, HEIGHT, TILE_COLS, CHANNELS), 1.0, 6.0, ((2, 16),)),
        "loss_grad": noise(splits[5], (TICK_COUNT, 2, HEIGHT, TILE_COLS, CHANNELS), 1.0, 6.0, ((2, 16),)),
    }


def activate(values):
    return jax.nn.silu(values.astype(jnp.float32)).astype(jnp.bfloat16)


def silu_slope(values):
    sigmoid = jax.nn.sigmoid(values)
    return sigmoid * (1.0 + values * (1.0 - sigmoid))


def rows_padded(field):
    return jnp.pad(field, ((1, 1), (0, 0), (0, 0)))


def gather_taps(rowpadded, flipped):
    height = rowpadded.shape[0] - 2
    across = rowpadded.shape[1]
    padded = jnp.pad(rowpadded, ((0, 0), (1, 1), (0, 0)))
    pieces = []
    for first in range(3):
        for second in range(3):
            if flipped:
                row_start, col_start = 2 - first, 2 - second
            else:
                row_start, col_start = first, second
            pieces.append(padded[row_start:row_start + height, col_start:col_start + across, :])
    return jnp.concatenate(pieces, -1).reshape(height * across, -1)


def apply_taps(taps_matrix, weight):
    return jnp.dot(taps_matrix, weight, preferred_element_type=jnp.float32)


def flip_weight(weight, channels):
    return weight.reshape(9, channels, channels).transpose(0, 2, 1).reshape(9 * channels, channels)


def correlate(taps_matrix, grads):
    return lax.dot_general(taps_matrix, grads, (((0,), (0,)), ((), ())), preferred_element_type=jnp.float32)


def forward_block(inputs, weight_f, weight_g):
    first_in, second_in = inputs[0], inputs[1]
    shape = first_in.shape
    taps_f = gather_taps(rows_padded(activate(second_in)), False)
    first_out = (first_in.astype(jnp.float32) + apply_taps(taps_f, weight_f).reshape(shape)).astype(jnp.bfloat16)
    taps_g = gather_taps(rows_padded(activate(first_out)), False)
    second_out = (second_in.astype(jnp.float32) + apply_taps(taps_g, weight_g).reshape(shape)).astype(jnp.bfloat16)
    return jnp.stack([first_out, second_out])


def backward_block(outputs, grads, weight_f, weight_g):
    first_out, second_out = outputs[0], outputs[1]
    first_grad, second_grad = grads[0], grads[1]
    shape = first_out.shape
    channels = shape[2]
    taps_g = gather_taps(rows_padded(activate(first_out)), False)
    second_in = (second_out.astype(jnp.float32) - apply_taps(taps_g, weight_g).reshape(shape)).astype(jnp.bfloat16)
    taps_f = gather_taps(rows_padded(activate(second_in)), False)
    first_in = (first_out.astype(jnp.float32) - apply_taps(taps_f, weight_f).reshape(shape)).astype(jnp.bfloat16)
    back_g = apply_taps(gather_taps(rows_padded(second_grad), True), flip_weight(weight_g, channels)).reshape(shape)
    first_back = (first_grad.astype(jnp.float32) + silu_slope(first_out.astype(jnp.float32)) * back_g).astype(jnp.bfloat16)
    back_f = apply_taps(gather_taps(rows_padded(first_back), True), flip_weight(weight_f, channels)).reshape(shape)
    second_back = (second_grad.astype(jnp.float32) + silu_slope(second_in.astype(jnp.float32)) * back_f).astype(jnp.bfloat16)
    grad_f = correlate(taps_f, first_back.reshape(-1, channels))
    grad_g = correlate(taps_g, second_grad.reshape(-1, channels))
    return jnp.stack([first_in, second_in]), jnp.stack([first_back, second_back]), jnp.stack([grad_f, grad_g])


def one_segment(pieces):
    state, outputs, grads, weight = pieces
    advanced = forward_block(state, weight[0], weight[1])
    inverted, backed, wgrad = backward_block(outputs, grads, weight[0], weight[1])
    return advanced, inverted, backed, wgrad


def reference(forward_state, returning_state, returning_grad, weights, fresh_input, loss_grad):
    totals = jnp.zeros((SEGMENTS, 2, 9 * CHANNELS, CHANNELS), jnp.float32)
    for tick_index in range(TICK_COUNT):
        advanced, inverted, backed, wgrad = lax.map(one_segment, (forward_state, returning_state, returning_grad, weights))
        totals = totals + wgrad
        forward_state = jnp.concatenate([fresh_input[tick_index][None], advanced[:-1]], 0)
        returning_state = jnp.concatenate([inverted[1:], advanced[-1:]], 0)
        returning_grad = jnp.concatenate([backed[1:], loss_grad[tick_index][None]], 0)
    return forward_state, returning_state, returning_grad, totals
```

```python
import functools

import jax
import jax.numpy as jnp
from jax import lax
from jax.experimental import pallas as pl
from jax.experimental.pallas import tpu as pltpu
from jax.sharding import PartitionSpec as P

F32 = jnp.float32
BF16 = jnp.bfloat16
VMEM = pl.BlockSpec(memory_space=pltpu.VMEM)
SMEM = pl.BlockSpec(memory_space=pltpu.SMEM)


def sigmoid(v):
    return 1.0 / (1.0 + jnp.exp(-v))


def act(v):
    v = v.astype(F32)
    return (v * sigmoid(v)).astype(BF16).astype(F32)


def slope(v):
    v = v.astype(F32)
    s = sigmoid(v)
    return s * (1.0 + v * (1.0 - s))


def stencil(x_ref, v, cols):
    n, ch = v.shape
    col = lax.rem(lax.broadcasted_iota(jnp.int32, (n, ch), 0), cols)
    x_ref[:, :ch] = jnp.where(col == 0, 0.0, pltpu.roll(v, 1, 0)).astype(BF16)
    x_ref[:, ch : 2 * ch] = v.astype(BF16)
    x_ref[:, 2 * ch :] = jnp.where(col == cols - 1, 0.0, pltpu.roll(v, n - 1, 0)).astype(BF16)


def conv(x_ref, w_ref, cols, start, size):
    depth = x_ref.shape[1]
    total = None
    for a in range(3):
        term = jnp.dot(
            x_ref[start + a * cols : start + a * cols + size, :],
            w_ref[a * depth : (a + 1) * depth, :],
            preferred_element_type=F32,
        )
        total = term if total is None else total + term
    return total


def correlate(x_ref, d, cols):
    size = d.shape[0]
    return [
        lax.dot_general(
            x_ref[a * cols : a * cols + size, :], d, (((0,), (0,)), ((), ())), preferred_element_type=F32
        )
        for a in range(3)
    ]


def stacked(*pieces):
    return jnp.concatenate([p.astype(F32) for p in pieces], axis=0)


def params(mib):
    return pltpu.CompilerParams(vmem_limit_bytes=mib << 20)


def estimate(matmuls, pixels, channels, extra):
    flops = matmuls * 2 * pixels * 9 * channels * channels
    return pl.CostEstimate(flops=flops, bytes_accessed=extra, transcendentals=4 * pixels * channels)


def invert_second(cols, tick, *refs):
    if tick == 0:
        (y_ref, g_ref, up_ref, down_ref, w_ref, wt_ref, out_ref, top_ref, bottom_ref, x_ref) = refs
        y1, y2, g1, g2 = (y_ref[0], y_ref[1], g_ref[0], g_ref[1])
    else:
        (flag_ref, came_ref, tops_ref, mids_ref, bots_ref, adv_ref, loss_ref, state_ref, up_ref, down_ref,
         w_ref, wt_ref, out_ref, top_ref, bottom_ref, y1g2_ref, x_ref) = refs
        local = flag_ref[0] == 1
        y1 = jnp.where(local, adv_ref[0], jnp.concatenate([tops_ref[0], mids_ref[0], bots_ref[0]], 0))
        g2 = jnp.where(local, loss_ref[1], jnp.concatenate([tops_ref[1], mids_ref[1], bots_ref[1]], 0))
        y2 = jnp.where(local, adv_ref[1], came_ref[0])
        g1 = jnp.where(local, loss_ref[0], came_ref[1])
        y1g2_ref[0] = y1
        y1g2_ref[1] = g2
    size = y1.shape[0]
    stencil(x_ref, act(stacked(up_ref[0], y1, down_ref[0])), cols)
    q2 = (y2.astype(F32) - conv(x_ref, w_ref, cols, 0, size)).astype(BF16)
    out_ref[0] = q2
    stencil(x_ref, stacked(up_ref[1], g2, down_ref[1]), cols)
    h1 = (g1.astype(F32) + slope(y1) * conv(x_ref, wt_ref, cols, 0, size)).astype(BF16)
    out_ref[1] = h1
    top_ref[0] = q2[:cols]
    top_ref[1] = h1[:cols]
    bottom_ref[0] = q2[size - cols :]
    bottom_ref[1] = h1[size - cols :]
    if tick:
        top_ref[2] = state_ref[1, :cols]
        bottom_ref[2] = state_ref[1, size - cols :]


def invert_first(cols, tick, *refs):
    if tick == 0:
        y_ref, g_ref, qh_ref, up_ref, down_ref, w_ref, wt_ref, tops_ref, mids_ref, bots_ref, x_ref = refs
        y1, g2 = (y_ref[0], g_ref[1])
    else:
        flag_ref, yg_ref, loss_ref, qh_ref, up_ref, down_ref, w_ref, wt_ref, p_ref, h_ref, x_ref = refs
        y1, g2 = (yg_ref[0], yg_ref[1])
    q2, h1 = (qh_ref[0], qh_ref[1])
    size = y1.shape[0]
    stencil(x_ref, act(stacked(up_ref[0], q2, down_ref[0])), cols)
    p2 = (y1.astype(F32) - conv(x_ref, w_ref, cols, 0, size)).astype(BF16)
    stencil(x_ref, stacked(up_ref[1], h1, down_ref[1]), cols)
    h2 = (g2.astype(F32) + slope(q2) * conv(x_ref, wt_ref, cols, 0, size)).astype(BF16)
    if tick == 0:
        for k, v in enumerate((p2, h2)):
            tops_ref[k] = v[:cols]
            mids_ref[k] = v[cols : size - cols]
            bots_ref[k] = v[size - cols :]
    else:
        first = flag_ref[1] == 1
        p_ref[...] = p2
        h_ref[0] = jnp.where(first, loss_ref[0], h1)
        h_ref[1] = jnp.where(first, loss_ref[1], h2)


def advance_first(cols, index, state_ref, up_ref, down_ref, w_ref, out_ref, top_ref, bottom_ref, x_ref):
    size = out_ref.shape[0]
    stencil(x_ref, act(stacked(up_ref[index], state_ref[1], down_ref[index])), cols)
    out = (state_ref[0].astype(F32) + conv(x_ref, w_ref, cols, 0, size)).astype(BF16)
    out_ref[...] = out
    top_ref[...] = out[:cols]
    bottom_ref[...] = out[size - cols :]


def advance_second(cols, flag_ref, state_ref, fresh_ref, first_ref, up_ref, down_ref, w_ref, adv_ref, send_ref, x_ref):
    size = first_ref.shape[0]
    stencil(x_ref, act(stacked(up_ref[...], first_ref[...], down_ref[...])), cols)
    out = (state_ref[1].astype(F32) + conv(x_ref, w_ref, cols, 0, size)).astype(BF16)
    last = flag_ref[0] == 1
    adv_ref[0] = first_ref[...]
    adv_ref[1] = out
    send_ref[0] = jnp.where(last, fresh_ref[0], first_ref[...])
    send_ref[1] = jnp.where(last, fresh_ref[1], out)


def weight_terms(cols, y_ref, g_ref, up1_ref, down1_ref, qh_ref, up2_ref, down2_ref, out_ref, x_ref):
    depth = x_ref.shape[1]
    stencil(x_ref, act(stacked(up2_ref[0], qh_ref[0], down2_ref[0])), cols)
    for a, term in enumerate(correlate(x_ref, qh_ref[1], cols)):
        out_ref[0, a * depth : (a + 1) * depth] = term
    stencil(x_ref, act(stacked(up1_ref[0], y_ref[0], down1_ref[0])), cols)
    for a, term in enumerate(correlate(x_ref, g_ref[1], cols)):
        out_ref[1, a * depth : (a + 1) * depth] = term


def weight_sums(cols, flag_ref, yg_ref, up1_ref, down1_ref, qh_ref, up2_ref, down2_ref, before_ref,
                send_ref, keep_ref, x_ref, total_ref):
    depth = x_ref.shape[1]
    core = flag_ref[4]
    rows = send_ref.shape[2]
    for k, (up, v, down, d) in enumerate((
        (up2_ref[0], qh_ref[0], down2_ref[0], qh_ref[1]),
        (up1_ref[0], yg_ref[0], down1_ref[0], yg_ref[1]),
    )):
        stencil(x_ref, act(stacked(up, v, down)), cols)
        for a, term in enumerate(correlate(x_ref, d, cols)):
            part = slice(a * depth, (a + 1) * depth)
            total_ref[part] = term + before_ref[k, part]
        for j in range(send_ref.shape[1]):
            mine = pl.multiple_of((2 * j + core) * rows, rows)
            other = pl.multiple_of((2 * j + 1 - core) * rows, rows)
            keep_ref[k, j] = total_ref[pl.ds(mine, rows)]
            send_ref[k, j] = total_ref[pl.ds(other, rows)].astype(BF16)


def sum_cores(flag_ref, keep_ref, came_ref, own_ref, right_ref, far_ref, left_ref):
    x = flag_ref[3]
    for d, ref in enumerate((own_ref, right_ref, far_ref, left_ref)):
        to = lax.rem(x + d, 4)
        for k in range(2):
            for z in range(2):
                value = keep_ref[k, 4 * z + to] + came_ref[k, 4 * z + to].astype(F32)
                ref[k, z] = value.astype(ref.dtype)


def sum_chips(flag_ref, own_ref, a_ref, b_ref, c_ref, keep_ref, send_ref):
    z = flag_ref[2]
    for k in range(2):
        for ref, at in ((keep_ref, z), (send_ref, 1 - z)):
            value = own_ref[k, at] + a_ref[k, at].astype(F32) + b_ref[k, at].astype(F32) + c_ref[k, at].astype(F32)
            ref[k] = value.astype(ref.dtype)


def shape(*dims, dtype=BF16):
    return jax.ShapeDtypeStruct(dims, dtype)


def call(body, n_scalars, args, outs, scratch, cost, mib=40, name=None):
    return pl.pallas_call(
        body,
        out_shape=outs,
        in_specs=[SMEM] * n_scalars + [VMEM] * (len(args) - n_scalars),
        out_specs=jax.tree.map(lambda _: VMEM, outs),
        scratch_shapes=scratch,
        compiler_params=params(mib),
        cost_estimate=cost,
        name=name,
    )(*args)


def flip(weight, channels):
    return weight.reshape(9, channels, channels)[::-1].transpose(0, 2, 1).reshape(9 * channels, channels)


def local(forward_state, returning_state, returning_grad, weights, fresh_input, loss_grad):
    rows, cols, ch = forward_state.shape[3 - 1 :]
    size = rows * cols
    segments = lax.axis_size("segment")
    bands = lax.axis_size("band")
    seg = lax.axis_index("segment")
    band = lax.axis_index("band")
    flags = jnp.stack([
        (seg == segments - 1).astype(jnp.int32),
        (seg == 0).astype(jnp.int32),
        band // 8,
        (band // 2) % 4,
        band % 2,
    ]).astype(jnp.int32)

    def up_down(bottom, top):
        return (
            lax.ppermute(bottom, "band", [(i, i + 1) for i in range(bands - 1)]),
            lax.ppermute(top, "band", [(i + 1, i) for i in range(bands - 1)]),
        )

    back_route = [(i + 1, i) for i in range(segments - 1)]
    back_ring = [(i, (i - 1) % segments) for i in range(segments)]
    ahead_ring = [(i, (i + 1) % segments) for i in range(segments)]

    def along(block, route):
        return lax.ppermute(block, "segment", route)

    state = forward_state.reshape(2, size, ch)
    y = returning_state.reshape(2, size, ch)
    g = returning_grad.reshape(2, size, ch)
    fresh = fresh_input.reshape(2, 2, size, ch)
    loss = loss_grad.reshape(2, 2, size, ch)
    w_f, w_g = (weights[0, 0], weights[0, 1])
    t_f, t_g = (flip(w_f, ch), flip(w_g, ch))
    x_scratch = [pltpu.VMEM((size + 2 * cols, 3 * ch), BF16)]
    MB = size * ch * 2
    WB = 9 * ch * ch * 2
    cost1 = estimate(1, size, ch, 3 * MB + WB)
    cost2 = estimate(2, size, ch, 6 * MB + 2 * WB)
    last = size - cols
    pair = shape(2, size, ch)
    edge2 = shape(2, cols, ch)
    edge3 = shape(3, cols, ch)

    e1 = up_down(
        jnp.stack([y[0, last:], g[1, last:], state[1, last:]]),
        jnp.stack([y[0, :cols], g[1, :cols], state[1, :cols]]),
    )
    qh, top, bottom = call(
        functools.partial(invert_second, cols, 0), 0, (y, g, *e1, w_g, t_g), (pair, edge2, edge2), x_scratch, cost2,
        name="invert_second",
    )
    came_qh = along(qh, back_route)
    e2 = up_down(bottom, top)
    tops, mids, bots = call(
        functools.partial(invert_first, cols, 0), 0, (y, g, qh, *e2, w_f, t_f),
        (edge2, shape(2, size - 2 * cols, ch), edge2), x_scratch, cost2, name="invert_first",
    )
    came_tops = along(tops, back_route)
    came_bots = along(bots, back_route)
    came_mids = along(mids, back_route)
    first, top, bottom = call(
        functools.partial(advance_first, cols, 2), 0, (state, *e1, w_f),
        (shape(size, ch), shape(cols, ch), shape(cols, ch)), x_scratch, cost1, name="advance_first",
    )
    e3 = up_down(bottom, top)
    adv, send = call(
        functools.partial(advance_second, cols), 1, (flags, state, fresh[0], first, *e3, w_g),
        (pair, pair), x_scratch, cost1, name="advance_second",
    )
    state = along(send, ahead_ring)
    terms = call(
        functools.partial(weight_terms, cols), 0, (y, g, *e1, qh, *e2), shape(2, 9 * ch, ch, dtype=F32),
        x_scratch, cost2, name="weight_terms",
    )

    at_end = seg == segments - 1
    f1 = up_down(
        jnp.where(at_end, jnp.stack([adv[0, last:], loss[0, 1, last:]]), came_bots),
        jnp.where(at_end, jnp.stack([adv[0, :cols], loss[0, 1, :cols]]), came_tops),
    )
    qh, top, bottom, yg = call(
        functools.partial(invert_second, cols, 1), 1,
        (flags, came_qh, came_tops, came_mids, came_bots, adv, loss[0], state, *f1, w_g, t_g),
        (pair, edge3, edge3, pair), x_scratch, cost2, name="invert_second",
    )
    q_out = along(qh[0], back_route)
    f2 = up_down(bottom, top)
    p2, hh = call(
        functools.partial(invert_first, cols, 1), 1, (flags, yg, loss[1], qh, *f2, w_f, t_f),
        (shape(size, ch), pair), x_scratch, cost2, name="invert_first",
    )
    p_out = along(p2, back_route)
    backward_out = along(hh, back_ring)
    send, keep = call(
        functools.partial(weight_sums, cols), 1, (flags, yg, *f1, qh, *f2, terms),
        (shape(2, 8, 9 * ch // bands, ch), shape(2, 8, 9 * ch // bands, ch, dtype=F32)),
        x_scratch + [pltpu.VMEM((9 * ch, ch), F32)], cost2, name="weight_sums",
    )
    first, top, bottom = call(
        functools.partial(advance_first, cols, 2), 0, (state, *f2, w_f),
        (shape(size, ch), shape(cols, ch), shape(cols, ch)), x_scratch, cost1, name="advance_first",
    )
    f3 = up_down(bottom, top)
    adv, ahead = call(
        functools.partial(advance_second, cols), 1, (flags, state, fresh[1], first, *f3, w_g),
        (pair, pair), x_scratch, cost1, name="advance_second",
    )
    forward_out = along(ahead, ahead_ring)

    part = 9 * ch // bands
    came = lax.ppermute(send, "band", [(i, i ^ 1) for i in range(bands)])

    def on_x(block, step):
        return lax.ppermute(
            block, "band", [(i, (i & 8) | ((((i >> 1) & 3) + step) % 4) << 1 | (i & 1)) for i in range(bands)]
        )

    quarter = shape(2, 2, part, ch)
    own, right, far, left = call(
        sum_cores, 1, (flags, keep, came), (shape(2, 2, part, ch, dtype=F32), quarter, quarter, quarter), [],
        estimate(0, size, ch, 8 * MB), name="sum_cores",
    )
    far, right, left = (on_x(far, 2), on_x(right, 1), on_x(left, 3))
    keep, send = call(
        sum_chips, 1, (flags, own, far, right, left), (shape(2, part, ch, dtype=F32), shape(2, part, ch)), [],
        estimate(0, size, ch, 3 * MB), name="sum_chips",
    )
    weight_grad = keep + lax.ppermute(send, "band", [(i, i ^ 8) for i in range(bands)]).astype(F32)

    returning_out = jnp.where(at_end, adv, jnp.stack([p_out, q_out]))
    full = forward_state.shape
    return (forward_out.reshape(full), returning_out.reshape(full), backward_out.reshape(full), weight_grad[None])


def solution(mesh):
    return jax.shard_map(
        local,
        mesh=mesh,
        in_specs=(
            P("segment", None, "band", None, None),
            P("segment", None, "band", None, None),
            P("segment", None, "band", None, None),
            P("segment", None, None, None),
            P(None, None, "band", None, None),
            P(None, None, "band", None, None),
        ),
        out_specs=(
            P("segment", None, "band", None, None),
            P("segment", None, "band", None, None),
            P("segment", None, "band", None, None),
            P("segment", None, "band", None),
        ),
        check_vma=False,
    )
```

```python
import functools

import jax
import jax.numpy as jnp
from jax import lax
from jax.experimental import pallas as pl
from jax.experimental.pallas import tpu as pltpu
from jax.sharding import PartitionSpec as P

F32 = jnp.float32
BF16 = jnp.bfloat16
ANY = pl.BlockSpec(memory_space=pl.ANY)
VMEM = pl.BlockSpec(memory_space=pltpu.VMEM)
SMEM = pl.BlockSpec(memory_space=pltpu.SMEM)
LITTLE = pl.CostEstimate(flops=1000, bytes_accessed=1000, transcendentals=0)


def shape(*dims, dtype=BF16):
    return jax.ShapeDtypeStruct(dims, dtype)


def last_section(at_ref):
    return at_ref[0] == at_ref[2] - 1


class View:
    def __init__(self, pieces, at_ref):
        self.pieces, self.at_ref = (pieces, at_ref)

    @property
    def ref(self):
        return self.pieces[0][0]

    def value(self):
        groups = []
        for ref, when in self.pieces:
            if when is None or not groups or groups[-1][0] is None:
                groups.append((None, [ref[...]]) if when is None else (0, ([], [])))
            if when is not None:
                groups[-1][1][int(when)].append(ref[...])
        parts = []
        for kind, group in groups:
            if kind is None:
                parts += group
            else:
                rest, last = (jnp.concatenate(g, 0) if len(g) > 1 else g[0] for g in group)
                parts.append(jnp.where(last_section(self.at_ref), last, rest))
        return parts[0] if len(parts) == 1 else jnp.concatenate(parts, 0)


def kernel(body, at, args, outs, scratch=(), after=(), mib=16):
    arrays = []

    def place(array):
        for i, a in enumerate(arrays):
            if a is array:
                return i
        arrays.append(array)
        return len(arrays) - 1

    plan = []
    for arg in args:
        if not isinstance(arg, list):
            arg = [(*(arg if isinstance(arg, tuple) else (arg, None)), None, None, None)]
        plan.append([(place(piece[0]), *piece[1:]) for piece in arg])
    after = [a for a in after if not any(a is b for b in arrays)]

    def run(*refs):
        at_ref, refs = (refs[len(after)], refs[len(after) + 1 :])
        views = []
        for pieces in plan:
            taken = []
            for i, index, start, size, when in pieces:
                ref = refs[i] if index is None else refs[i].at[index]
                taken.append((ref if start is None else ref.at[pl.ds(start, size)], when))
            views.append(View(taken, at_ref))
        refs = refs[len(arrays) :]
        body(at_ref, views, refs[: len(outs)], refs[len(outs) :])

    return pl.pallas_call(
        run,
        out_shape=outs,
        in_specs=[ANY] * len(after) + [SMEM] + [VMEM] * len(arrays),
        out_specs=[VMEM] * len(outs),
        scratch_shapes=list(scratch),
        compiler_params=pltpu.CompilerParams(vmem_limit_bytes=mib << 20),
        cost_estimate=LITTLE,
        name=getattr(body, "func", body).__name__,
    )(*after, at, *arrays)


def sigmoid(v):
    return 1.0 / (1.0 + jnp.exp(-v))


def act(v):
    v = v.astype(F32)
    return (v * sigmoid(v)).astype(BF16).astype(F32)


def slope(v):
    v = v.astype(F32)
    s = sigmoid(v)
    return s * (1.0 + v * (1.0 - s))


def stencil(x_ref, v, cols):
    n, ch = v.shape
    v = v.astype(F32)
    col = lax.rem(lax.broadcasted_iota(jnp.int32, (n, ch), 0), cols)
    x_ref[:n, :ch] = jnp.where(col == 0, 0.0, pltpu.roll(v, 1, 0)).astype(BF16)
    x_ref[:n, ch : 2 * ch] = v.astype(BF16)
    x_ref[:n, 2 * ch :] = jnp.where(col == cols - 1, 0.0, pltpu.roll(v, n - 1, 0)).astype(BF16)


def conv(x_ref, w_ref, cols, size):
    depth = x_ref.shape[1]
    total = None
    for a in range(3):
        term = jnp.dot(
            x_ref[a * cols : a * cols + size, :], w_ref[a * depth : (a + 1) * depth, :], preferred_element_type=F32
        )
        total = term if total is None else total + term
    return total


def correlate(x_ref, d, cols):
    size = d.shape[0]
    return [
        lax.dot_general(
            x_ref[a * cols : a * cols + size, :], d, (((0,), (0,)), ((), ())), preferred_element_type=F32
        )
        for a in range(3)
    ]


def inside_image(at_ref, values, margin):
    n = values.shape[0]
    pixel = lax.broadcasted_iota(jnp.int32, values.shape, 0)
    low = jnp.where(at_ref[1] == 0, margin, 0)
    high = jnp.where(at_ref[1] == at_ref[3] - 1, n - margin, n)
    return jnp.where((pixel >= low) & (pixel < high), values, jnp.zeros_like(values))


def flip(at_ref, args, outs, own):
    w_ref = args[0].ref
    ch = w_ref.shape[2]
    for k in (1, 0):
        for t in range(9):
            outs[0][k, (8 - t) * ch : (9 - t) * ch, :] = w_ref[k, t * ch : (t + 1) * ch, :].T


def pack(*refs):
    ins, outs = (refs[:-2], refs[-2:])
    half = len(ins) // 2
    for group, out in ((ins[:half], outs[0]), (ins[half:], outs[1])):
        end = 0
        for ref in group:
            size = ref.shape[-2]
            out[end : end + size] = ref[...].reshape(size, ref.shape[-1])
            end += size


def pick(at_ref, args, outs, own):
    for k, out in enumerate(outs):
        end = 0
        for arg in args[k * len(args) // len(outs) : (k + 1) * len(args) // len(outs)]:
            value = arg.value()
            out[end : end + value.shape[0]] = value
            end += value.shape[0]


def invert(cols, tick, at_ref, args, outs, own):
    y1, g2, y2, g1, w_f, w_g, t_f, t_g = args[:8]
    x_ref = own[0]
    y1, g2 = (y1.value(), g2.value())
    edge = 2 * cols
    wide = y1.shape[0] - edge
    size = wide - edge
    stencil(x_ref, act(y1), cols)
    q2 = (y2.value().astype(F32) - conv(x_ref, w_g.ref, cols, wide)).astype(BF16)
    q2 = inside_image(at_ref, q2, cols)
    outs[0][...] = q2
    stencil(x_ref, g2, cols)
    back = conv(x_ref, t_g.ref, cols, wide)
    h1 = (g1.value().astype(F32) + slope(y1[cols : cols + wide]) * back).astype(BF16)
    h1 = inside_image(at_ref, h1, cols)
    outs[1][...] = h1
    stencil(x_ref, act(q2), cols)
    p2 = (y1[edge : edge + size].astype(F32) - conv(x_ref, w_f.ref, cols, size)).astype(BF16)
    here = slice(cols, cols + size)
    stencil(x_ref, h1, cols)
    back = conv(x_ref, t_f.ref, cols, size)
    q2, h1 = (q2[here], h1[here])
    h2 = (g2[edge : edge + size].astype(F32) + slope(q2) * back).astype(BF16)
    if tick == 1:
        first = at_ref[0] == 0
        out, y_out, g_out = outs[2:]
        loss = args[8].ref
        out[0] = p2
        out[1] = q2
        out[2] = jnp.where(first, loss[0], h1)
        out[3] = jnp.where(first, loss[1], h2)
        y_out[...] = y1[cols : cols + wide]
        g_out[...] = g2[edge : edge + size]
    else:
        top, bottom = outs[2:4]
        inner = size - 2 * edge
        for k, (two, one) in enumerate(((p2, q2), (h2, h1))):
            at = k * edge
            top[at : at + edge] = two[:edge]
            bottom[at : at + edge] = two[size - edge :]
            at = 2 * edge + k * cols
            top[at : at + cols] = one[:cols]
            bottom[at : at + cols] = one[size - cols :]
            outs[4 + k][:inner] = two[edge : size - edge]
            outs[4 + k][inner:] = one[cols : size - cols]


def advance(cols, extra, at_ref, args, outs, own):
    q, p, w_f, w_g, new_q, new_p = args[:6]
    x_ref = own[0]
    q = q.value()
    edge = 2 * cols
    wide = q.shape[0] - edge
    size = wide - edge
    margin = extra * cols
    stencil(x_ref, act(q), cols)
    out1 = (p.value().astype(F32) + conv(x_ref, w_f.ref, cols, wide)).astype(BF16)
    out1 = inside_image(at_ref, out1, margin + cols)
    stencil(x_ref, act(out1), cols)
    out2 = (q[edge : edge + size].astype(F32) + conv(x_ref, w_g.ref, cols, size)).astype(BF16)
    adv, send = outs[:2]
    here = size - 2 * margin
    adv[0] = out1[cols + margin : cols + margin + here]
    adv[1] = out2[margin : margin + here]
    last = last_section(at_ref)
    if extra:
        out2 = inside_image(at_ref, out2, margin)
        send[:size] = jnp.where(last, new_q.value(), out2)
        rest = out1[margin : margin + here + edge]
        send[size:] = jnp.where(last, new_p.value(), rest)
        outs[2][...] = args[6].ref[...]
        outs[3][...] = args[7].ref[...]
    else:
        send[0] = jnp.where(last, new_p.value(), adv[0])
        send[1] = jnp.where(last, new_q.value(), out2)


def weight_terms(cols, at_ref, args, outs, own):
    x_ref = own[0]
    depth = x_ref.shape[1]
    for k, (v, d) in enumerate((args[2:4], args[0:2])):
        stencil(x_ref, act(v.value()), cols)
        for a, term in enumerate(correlate(x_ref, d.value(), cols)):
            outs[0][k, a * depth : (a + 1) * depth] = term


def weight_sums(cols, at_ref, args, outs, own):
    x_ref, total = own
    depth = x_ref.shape[1]
    even = lax.rem(at_ref[1], 2) == 0
    keep, send = outs
    rows = send.shape[2]
    before = args[4].ref
    for k, (v, d) in enumerate((args[2:4], args[0:2])):
        stencil(x_ref, act(v.value()), cols)
        for a, term in enumerate(correlate(x_ref, d.value(), cols)):
            part = slice(a * depth, (a + 1) * depth)
            total[part] = term + before[k, part]
        for j in range(send.shape[1]):
            one = total[2 * j * rows : (2 * j + 1) * rows]
            two = total[(2 * j + 1) * rows : (2 * j + 2) * rows]
            keep[k, j] = jnp.where(even, one, two)
            send[k, j] = jnp.where(even, two, one).astype(BF16)


def sum_cores(at_ref, args, outs, own):
    keep, came = (arg.ref for arg in args)
    x = lax.rem(at_ref[1] // 2, 4)
    for d, out in zip((0, 2, 1, 3), outs):
        to = lax.rem(x + d, 4)
        for k in range(2):
            for z in range(2):
                out[k, z] = (keep[k, 4 * z + to] + came[k, 4 * z + to].astype(F32)).astype(out.dtype)


def sum_chips(at_ref, args, outs, own):
    z = at_ref[1] // 8
    parts = [arg.ref for arg in args]
    for k in range(2):
        for out, at in ((outs[0], 1 - z), (outs[1], z)):
            value = parts[0][k, at]
            for part in parts[1:]:
                value = value + part[k, at].astype(F32)
            out[k] = value.astype(out.dtype)


def place_outputs(at_ref, ahead_ref, back_ref, adv_ref, forward_ref, returning_ref, backward_ref, sem):
    last = last_section(at_ref)
    ahead = pltpu.make_async_copy(ahead_ref, forward_ref, sem.at[0])
    back = pltpu.make_async_copy(back_ref.at[pl.ds(2, 2)], backward_ref, sem.at[1])
    came = pltpu.make_async_copy(back_ref.at[pl.ds(0, 2)], returning_ref, sem.at[2])
    own = pltpu.make_async_copy(adv_ref, returning_ref, sem.at[2])
    ahead.start()
    back.start()
    pl.when(last)(own.start)
    pl.when(jnp.logical_not(last))(came.start)
    ahead.wait()
    back.wait()
    came.wait()


def local(forward_state, returning_state, returning_grad, weights, fresh_input, loss_grad):
    full = forward_state.shape
    rows, cols, ch = full[2:]
    size = rows * cols
    edge = 2 * cols
    segments = lax.axis_size("segment")
    bands = lax.axis_size("band")
    seg = lax.axis_index("segment")
    at = jnp.stack([seg, lax.axis_index("band"), segments, bands]).astype(jnp.int32)

    def up_down(bottom, top):
        return (
            lax.ppermute(bottom, "band", [(i, i + 1) for i in range(bands - 1)]),
            lax.ppermute(top, "band", [(i + 1, i) for i in range(bands - 1)]),
        )

    back_route = [(i + 1, i) for i in range(segments - 1)]
    back_ring = [(i, (i - 1) % segments) for i in range(segments)]
    ahead_ring = [(i, (i + 1) % segments) for i in range(segments)]

    def along(block, route):
        return lax.ppermute(block, "segment", route)

    state = forward_state.reshape(2, size, ch)
    y = returning_state.reshape(2, size, ch)
    g = returning_grad.reshape(2, size, ch)
    fresh = fresh_input.reshape(4, size, ch)
    loss = loss_grad.reshape(2, 2, size, ch)
    w = weights[0]
    w_f, w_g = ((w, 0), (w, 1))

    def x_scratch(extra):
        return pltpu.VMEM((size + 2 * extra * cols, 3 * ch), BF16)

    pair = shape(2, size, ch)
    ext = shape(size + edge, ch)
    e6 = shape(6 * cols, ch)

    def pack_edges(parts):
        count = sum(n for _, _, n in parts) * cols

        def spec(index, n, last):
            start = (rows - n) * cols if last else 0
            return pl.BlockSpec((pl.Element(1), pl.Element(n * cols), pl.Element(ch)), lambda i: (index, start, 0))

        return pl.pallas_call(
            pack, grid=(1,), out_shape=[shape(count, ch)] * 2,
            in_specs=[spec(index, n, last) for last in (True, False) for _, index, n in parts],
            out_specs=[pl.BlockSpec((count, ch), lambda i: (0, 0))] * 2,
            compiler_params=pltpu.CompilerParams(vmem_limit_bytes=60 << 20), cost_estimate=LITTLE, name="pack_edges",
        )(*[array for array, _, _ in parts] * 2)

    up, down = up_down(*pack_edges([(y, 0, 2), (g, 1, 2), (y, 1, 1), (g, 0, 1), (fresh, 1, 2), (fresh, 0, 1)]))
    fwd_up, fwd_down = up_down(*pack_edges([(state, 1, 4), (state, 0, 3)]))
    (w_t,) = kernel(flip, at, (w,), (shape(2, 9 * ch, ch),))

    def extended(start, n, middle, up, down):
        start, n = (start * cols, n * cols)
        return [(up, None, start, n, None), *middle, (down, None, start, n, None)]

    def all_of(array, index):
        return [(array, index, 0, size, None)]

    mid = shape(2 * size - 6 * cols, ch)
    q2, h1, top, bottom, mid_y, mid_g = kernel(
        functools.partial(invert, cols, 0), at,
        (
            extended(0, 2, all_of(y, 0), up, down), extended(2, 2, all_of(g, 1), up, down),
            extended(4, 1, all_of(y, 1), up, down), extended(5, 1, all_of(g, 0), up, down),
            w_f, w_g, (w_t, 0), (w_t, 1),
        ),
        (ext, ext, e6, e6, mid, mid), [x_scratch(2)], (),
    )
    came_bottom = along(bottom, back_route)
    came_top = along(top, back_route)
    adv, ahead, mid_y, mid_g = kernel(
        functools.partial(advance, cols, 2), at,
        (
            extended(0, 4, all_of(state, 1), fwd_up, fwd_down), extended(4, 3, all_of(state, 0), fwd_up, fwd_down),
            w_f, w_g,
            extended(6, 2, all_of(fresh, 1), up, down), extended(8, 1, all_of(fresh, 0), up, down), mid_y, mid_g,
        ),
        (pair, shape(2 * size + 6 * cols, ch), mid, mid), [x_scratch(4)], (top,),
    )
    came_mids = (along(mid_y, back_route), along(mid_g, back_route))
    state = along(ahead, ahead_ring)
    (terms,) = kernel(
        functools.partial(weight_terms, cols), at,
        (
            [(up, None, cols, cols, None), (y, 0, 0, size, None), (down, None, 0, cols, None)], (g, 1),
            q2, [(h1, None, cols, size, None)],
        ),
        (shape(2, 9 * ch, ch, dtype=F32),), [x_scratch(1)], (adv,),
    )
    (w_t,) = kernel(flip, at, (w,), (shape(2, 9 * ch, ch),), after=(terms,))

    spans = ((0, 2, adv, 0), (2, 2, loss, (0, 1)), (4, 1, adv, 1), (5, 1, loss, (0, 0)))
    picks = [
        [
            (came, None, start * cols, n * cols, False),
            (own, index, size - n * cols if came is came_bottom else 0, n * cols, True),
        ]
        for came in (came_bottom, came_top)
        for start, n, own, index in spans
    ]
    bottom, top = kernel(pick, at, picks, (e6, e6))
    up, down = up_down(bottom, top)
    inner, outer = (size - 2 * edge, size - edge)

    def came_field(k):
        start, n, own, index = spans[k]
        mid = came_mids[k % 2]
        return extended(start, n, [
            (came_top, None, start * cols, n * cols, False),
            (mid, None, 0, inner, False) if k < 2 else (mid, None, inner, outer, False),
            (came_bottom, None, start * cols, n * cols, False), (own, index, 0, size, True),
        ], up, down)

    q2, h1, back, y1, g2 = kernel(
        functools.partial(invert, cols, 1), at,
        (
            *[came_field(k) for k in range(4)], w_f, w_g, (w_t, 0), (w_t, 1), (loss, 1),
        ),
        (ext, ext, shape(4, size, ch), ext, shape(size, ch)), [x_scratch(2)],
    )
    came_back = along(back, back_ring)
    part = 9 * ch // bands
    chunks = (2, 8, part, ch)
    keep, send = kernel(
        functools.partial(weight_sums, cols), at, (y1, g2, q2, [(h1, None, cols, size, None)], terms),
        (shape(*chunks, dtype=F32), shape(*chunks)), [x_scratch(1), pltpu.VMEM((9 * ch, ch), F32)], (back,),
    )
    adv, ahead = kernel(
        functools.partial(advance, cols, 0), at,
        (
            [(state, None, 0, size + 2 * edge, None)], [(state, None, size + 2 * edge, size + edge, None)], w_f, w_g,
            (fresh, 3), (fresh, 2),
        ),
        (pair, pair), [x_scratch(2)], (send,),
    )
    came_ahead = along(ahead, ahead_ring)

    def on_x(piece, step):
        return lax.ppermute(
            piece, "band", [(i, (i & 8) | ((((i >> 1) & 3) + step) % 4) << 1 | (i & 1)) for i in range(bands)]
        )

    def over_bands(send, keep, at):
        came = lax.ppermute(send, "band", [(i, i ^ 1) for i in range(bands)])
        quarter = shape(2, 2, part, ch)
        own, far, right, left = kernel(
            sum_cores, at, (keep, came), (shape(2, 2, part, ch, dtype=F32), quarter, quarter, quarter)
        )
        far, right, left = (on_x(far, 2), on_x(right, 1), on_x(left, 3))
        send, keep = kernel(
            sum_chips, at, (own, far, right, left), (shape(2, part, ch), shape(2, part, ch, dtype=F32))
        )
        return keep + lax.ppermute(send, "band", [(i, i ^ 8) for i in range(bands)]).astype(F32)

    send, keep, _ = lax.optimization_barrier((send, keep, adv))
    weight_grad = lax.cond(seg < segments, over_bands, lambda *_: jnp.zeros((2, part, ch), F32), send, keep, at)

    outputs = pl.pallas_call(
        place_outputs, out_shape=[pair] * 3, in_specs=[SMEM] + [VMEM] * 3, out_specs=[ANY] * 3,
        scratch_shapes=[pltpu.SemaphoreType.DMA((3,))], cost_estimate=LITTLE,
        compiler_params=pltpu.CompilerParams(vmem_limit_bytes=8 << 20), name="place_outputs",
    )(at, came_ahead, came_back, adv)
    return (*[out.reshape(full) for out in outputs], weight_grad[None])


def solution(mesh):
    return jax.shard_map(
        local,
        mesh=mesh,
        in_specs=(
            P("segment", None, "band", None, None),
            P("segment", None, "band", None, None),
            P("segment", None, "band", None, None),
            P("segment", None, None, None),
            P(None, None, "band", None, None),
            P(None, None, "band", None, None),
        ),
        out_specs=(
            P("segment", None, "band", None, None),
            P("segment", None, "band", None, None),
            P("segment", None, "band", None, None),
            P("segment", None, "band", None),
        ),
        check_vma=False,
    )
```

```python
import functools

import jax
import jax.numpy as jnp
from jax import lax
from jax.experimental import pallas as pl
from jax.experimental.pallas import tpu as pltpu
from jax.sharding import PartitionSpec as P

F32 = jnp.float32
BF16 = jnp.bfloat16
ANY = pl.BlockSpec(memory_space=pl.ANY)
VMEM = pl.BlockSpec(memory_space=pltpu.VMEM)
SMEM = pl.BlockSpec(memory_space=pltpu.SMEM)
LITTLE = pl.CostEstimate(flops=1000, bytes_accessed=1000, transcendentals=0)


def shape(*dims, dtype=BF16):
    return jax.ShapeDtypeStruct(dims, dtype)


def last_section(at_ref):
    return at_ref[0] == at_ref[2] - 1


def even_band(at_ref):
    return lax.rem(at_ref[1], 2) == 0


class View:
    def __init__(self, pieces, at_ref):
        self.pieces, self.at_ref = (pieces, at_ref)

    @property
    def ref(self):
        return self.pieces[0][0]

    def value(self):
        groups = []
        for ref, when in self.pieces:
            test, truth = when if when else (None, False)
            if not groups or groups[-1][0] is not test:
                groups.append((test, ([], [])))
            groups[-1][1][truth].append(ref[...])
        parts = []
        for test, group in groups:
            no, yes = (jnp.concatenate(g, 0) if len(g) > 1 else g[0] if g else None for g in group)
            parts.append(no if test is None else jnp.where(test(self.at_ref), yes, no))
        return parts[0] if len(parts) == 1 else jnp.concatenate(parts, 0)


def kernel(body, at, args, outs, scratch=(), after=(), token=False, mib=16):
    arrays = []
    outs = [*outs, shape(8, 128, dtype=F32)] if token else outs

    def place(array):
        for i, a in enumerate(arrays):
            if a is array:
                return i
        arrays.append(array)
        return len(arrays) - 1

    plan = []
    for arg in args:
        if not isinstance(arg, list):
            arg = [(*(arg if isinstance(arg, tuple) else (arg, None)), None, None, None)]
        plan.append([(place(piece[0]), *piece[1:]) for piece in arg])

    def run(*refs):
        at_ref, refs = (refs[len(after)], refs[len(after) + 1 :])
        views = []
        for pieces in plan:
            taken = []
            for i, index, start, size, when in pieces:
                ref = refs[i] if index is None else refs[i].at[index]
                taken.append((ref if start is None else ref.at[pl.ds(start, size)], when))
            views.append(View(taken, at_ref))
        refs = refs[len(arrays) :]
        body(at_ref, views, refs[: len(outs) - token], refs[len(outs) :])
        if token:
            refs[len(outs) - 1][...] = jnp.zeros((8, 128), F32)

    return pl.pallas_call(
        run,
        out_shape=outs,
        in_specs=[VMEM] * len(after) + [SMEM] + [VMEM] * len(arrays),
        out_specs=[VMEM] * len(outs),
        scratch_shapes=list(scratch),
        compiler_params=pltpu.CompilerParams(vmem_limit_bytes=mib << 20),
        cost_estimate=LITTLE,
        name=getattr(body, "func", body).__name__,
    )(*after, at, *arrays)


def sigmoid(v):
    return 1.0 / (1.0 + jnp.exp(-v))


def act(v):
    v = v.astype(F32)
    return (v * sigmoid(v)).astype(BF16).astype(F32)


def slope(v):
    v = v.astype(F32)
    s = sigmoid(v)
    return s * (1.0 + v * (1.0 - s))


def stencil(x_ref, v, cols):
    n, ch = v.shape
    v = v.astype(F32)
    col = lax.rem(lax.broadcasted_iota(jnp.int32, (n, ch), 0), cols)
    x_ref[:n, :ch] = jnp.where(col == 0, 0.0, pltpu.roll(v, 1, 0)).astype(BF16)
    x_ref[:n, ch : 2 * ch] = v.astype(BF16)
    x_ref[:n, 2 * ch :] = jnp.where(col == cols - 1, 0.0, pltpu.roll(v, n - 1, 0)).astype(BF16)


def conv(x_ref, w_ref, cols, size):
    depth = x_ref.shape[1]
    total = None
    for a in range(3):
        term = jnp.dot(
            x_ref[a * cols : a * cols + size, :], w_ref[a * depth : (a + 1) * depth, :], preferred_element_type=F32
        )
        total = term if total is None else total + term
    return total


def correlate(x_ref, d, cols):
    size = d.shape[0]
    return [
        lax.dot_general(
            x_ref[a * cols : a * cols + size, :], d, (((0,), (0,)), ((), ())), preferred_element_type=F32
        )
        for a in range(3)
    ]


def inside_image(at_ref, values, margin):
    n = values.shape[0]
    pixel = lax.broadcasted_iota(jnp.int32, values.shape, 0)
    low = jnp.where(at_ref[1] == 0, margin, 0)
    high = jnp.where(at_ref[1] == at_ref[3] - 1, n - margin, n)
    return jnp.where((pixel >= low) & (pixel < high), values, jnp.zeros_like(values))


def flip(at_ref, args, outs, own):
    w_ref = args[0].ref
    ch = w_ref.shape[2]
    for k in (1, 0):
        for t in range(9):
            outs[0][k, (8 - t) * ch : (9 - t) * ch, :] = w_ref[k, t * ch : (t + 1) * ch, :].T


def by_band(at_ref, bottom, top, inner_ref, outer_ref):
    even = even_band(at_ref)
    inner_ref[...] = jnp.where(even, bottom, top)
    outer_ref[...] = jnp.where(even, top, bottom)


def pack(counts, at_ref, *refs):
    refs, outs = (list(refs), refs[-2 * len(counts) :])
    for k, count in enumerate(counts):
        sides = []
        for _ in range(2):
            sides.append(jnp.concatenate([refs.pop(0)[0] for _ in range(count)], 0))
        by_band(at_ref, *sides, *outs[2 * k : 2 * k + 2])


def pick(at_ref, args, outs, own):
    half = len(args) // 2
    sides = [jnp.concatenate([arg.value() for arg in part], 0) for part in (args[:half], args[half:])]
    by_band(at_ref, *sides, *outs)


def invert_second(cols, x_ref, at_ref, y1, g2, y2, g1, w_g, t_g):
    wide = y1.shape[0] - 2 * cols
    stencil(x_ref, act(y1), cols)
    q2 = inside_image(at_ref, (y2.astype(F32) - conv(x_ref, w_g, cols, wide)).astype(BF16), cols)
    stencil(x_ref, g2, cols)
    back = conv(x_ref, t_g, cols, wide)
    h1 = (g1.astype(F32) + slope(y1[cols : cols + wide]) * back).astype(BF16)
    return q2, inside_image(at_ref, h1, cols)


def invert_first(cols, x_ref, y1, g2, q2, h1, w_f, t_f):
    size = y1.shape[0]
    stencil(x_ref, act(q2), cols)
    p2 = (y1.astype(F32) - conv(x_ref, w_f, cols, size)).astype(BF16)
    stencil(x_ref, h1, cols)
    back = conv(x_ref, t_f, cols, size)
    h2 = (g2.astype(F32) + slope(q2[cols : cols + size]) * back).astype(BF16)
    return p2, h2


def invert(cols, at_ref, args, outs, own):
    y1, g2, y2, g1 = (arg.value() for arg in args[:4])
    w_f, w_g, t_f, t_g = (arg.ref for arg in args[4:])
    edge = 2 * cols
    size = y1.shape[0] - 2 * edge
    q2, h1 = invert_second(cols, own[0], at_ref, y1, g2, y2, g1, w_g, t_g)
    outs[0][...] = q2
    outs[1][...] = h1
    there = slice(edge, edge + size)
    p2, h2 = invert_first(cols, own[0], y1[there], g2[there], q2, h1, w_f, t_f)
    here = slice(cols, cols + size)
    edges = outs[2]
    half = edges.shape[0] // 2
    inner = size - 2 * edge
    for k, (two, one) in enumerate(((p2, q2[here]), (h2, h1[here]))):
        at = k * edge
        edges[at : at + edge] = two[:edge]
        edges[half + at : half + at + edge] = two[size - edge :]
        at = 2 * edge + k * cols
        edges[at : at + cols] = one[:cols]
        edges[half + at : half + at + cols] = one[size - cols :]
        outs[3 + k][:inner] = two[edge : size - edge]
        outs[3 + k][inner:] = one[cols : size - cols]


def invert_last(cols, at_ref, args, outs, own):
    y1, g2, y2, g1 = (arg.value() for arg in args[:4])
    w_f, w_g, t_f, t_g, loss = (arg.ref for arg in args[4:])
    edge = 2 * cols
    size = y1.shape[0] - 2 * edge
    here = slice(cols, cols + size)
    there = slice(edge, edge + size)
    q2, h1 = invert_second(cols, own[0], at_ref, y1, g2, y2, g1, w_g, t_g)
    p2, h2 = invert_first(cols, own[0], y1[there], g2[there], q2, h1, w_f, t_f)
    send, fields = outs
    first = at_ref[0] == 0
    send[0] = p2
    send[1] = q2[here]
    send[2] = jnp.where(first, loss[0], h1[here])
    send[3] = jnp.where(first, loss[1], h2)
    inside = slice(cols, cols + size + edge)
    for k, field in enumerate((q2, h1, y1[inside], g2[inside])):
        fields[k] = field


def advance(cols, extra, at_ref, args, outs, own):
    q, p, w_f, w_g, new_q, new_p = args[:6]
    x_ref = own[0]
    q = q.value()
    edge = 2 * cols
    wide = q.shape[0] - edge
    size = wide - edge
    margin = extra * cols
    stencil(x_ref, act(q), cols)
    out1 = (p.value().astype(F32) + conv(x_ref, w_f.ref, cols, wide)).astype(BF16)
    out1 = inside_image(at_ref, out1, margin + cols)
    stencil(x_ref, act(out1), cols)
    out2 = (q[edge : edge + size].astype(F32) + conv(x_ref, w_g.ref, cols, size)).astype(BF16)
    adv, send = outs[:2]
    here = size - 2 * margin
    adv[0] = out1[cols + margin : cols + margin + here]
    adv[1] = out2[margin : margin + here]
    last = last_section(at_ref)
    if extra:
        out2 = inside_image(at_ref, out2, margin)
        send[...] = jnp.where(last, new_q.value(), out2)
        outs[2][...] = jnp.where(last, new_p.value(), out1[margin : margin + here + edge])
        outs[3][...] = args[6].ref[...]
        outs[4][...] = args[7].ref[...]
    else:
        send[0] = jnp.where(last, new_p.value(), adv[0])
        send[1] = jnp.where(last, new_q.value(), out2)


def weight_terms(cols, at_ref, args, outs, own):
    x_ref = own[0]
    depth = x_ref.shape[1]
    for k, (v, d) in enumerate((args[2:4], args[0:2])):
        stencil(x_ref, act(v.value()), cols)
        for a, term in enumerate(correlate(x_ref, d.value(), cols)):
            outs[0][k, a * depth : (a + 1) * depth] = term.astype(BF16)


def weight_sums(cols, at_ref, args, outs, own):
    x_ref, total = own
    depth = x_ref.shape[1]
    even = lax.rem(at_ref[1], 2) == 0
    keep, send = outs
    rows = send.shape[2]
    before = args[4].ref
    for k, (v, d) in enumerate((args[2:4], args[0:2])):
        stencil(x_ref, act(v.value()), cols)
        for a, term in enumerate(correlate(x_ref, d.value(), cols)):
            part = slice(a * depth, (a + 1) * depth)
            total[part] = term + before[k, part].astype(F32)
        for j in range(send.shape[1]):
            one = total[2 * j * rows : (2 * j + 1) * rows]
            two = total[(2 * j + 1) * rows : (2 * j + 2) * rows]
            keep[k, j] = jnp.where(even, one, two)
            send[k, j] = jnp.where(even, two, one).astype(BF16)


def sum_cores(at_ref, args, outs, own):
    keep, came = (arg.ref for arg in args)
    x = lax.rem(at_ref[1] // 2, 4)
    for d, out in zip((0, 2, 1, 3), outs):
        to = lax.rem(x + d, 4)
        for k in range(2):
            for z in range(2):
                out[k, z] = (keep[k, 4 * z + to] + came[k, 4 * z + to].astype(F32)).astype(out.dtype)


def sum_chips(at_ref, args, outs, own):
    z = at_ref[1] // 8
    parts = [arg.ref for arg in args]
    for k in range(2):
        for out, at in ((outs[0], 1 - z), (outs[1], z)):
            value = parts[0][k, at]
            for part in parts[1:]:
                value = value + part[k, at].astype(F32)
            out[k] = value.astype(out.dtype)


def place_outputs(at_ref, ahead_ref, back_ref, adv_ref, grad_ref,
                  forward_ref, returning_ref, backward_ref, weight_ref, held, sem):
    last = last_section(at_ref)
    copies = [
        pltpu.make_async_copy(ahead_ref, forward_ref, sem.at[0]),
        pltpu.make_async_copy(back_ref.at[pl.ds(2, 2)], backward_ref, sem.at[1]),
        pltpu.make_async_copy(grad_ref, weight_ref, sem.at[3]),
    ]
    came = pltpu.make_async_copy(back_ref.at[pl.ds(0, 2)], returning_ref, sem.at[2])
    for copy in copies:
        copy.start()
    pl.when(jnp.logical_not(last))(came.start)

    @pl.when(last)
    def own():
        fetch = pltpu.make_async_copy(adv_ref, held, sem.at[4])
        fetch.start()
        fetch.wait()
        pltpu.make_async_copy(held, returning_ref, sem.at[2]).start()

    for copy in copies:
        copy.wait()
    came.wait()


def local(forward_state, returning_state, returning_grad, weights, fresh_input, loss_grad):
    full = forward_state.shape
    rows, cols, ch = full[2:]
    size = rows * cols
    edge = 2 * cols
    segments = lax.axis_size("segment")
    bands = lax.axis_size("band")
    seg = lax.axis_index("segment")
    at = jnp.stack([seg, lax.axis_index("band"), segments, bands]).astype(jnp.int32)

    def swap(inner, outer):
        return (
            lax.ppermute(inner, "band", [(i, i ^ 1) for i in range(bands)]),
            lax.ppermute(outer, "band", [(i, i + 1 if i % 2 else i - 1) for i in range(1, bands - 1)]),
        )

    back_route = [(i + 1, i) for i in range(segments - 1)]
    back_ring = [(i, (i - 1) % segments) for i in range(segments)]
    ahead_ring = [(i, (i + 1) % segments) for i in range(segments)]

    def along(block, route):
        return lax.ppermute(block, "segment", route)

    state = forward_state.reshape(2, size, ch)
    y = returning_state.reshape(2, size, ch)
    g = returning_grad.reshape(2, size, ch)
    fresh = fresh_input.reshape(4, size, ch)
    loss = loss_grad.reshape(2, 2, size, ch)
    w = weights[0]
    w_f, w_g = ((w, 0), (w, 1))

    def x_scratch(extra):
        return pltpu.VMEM((size + 2 * extra * cols, 3 * ch), BF16)

    pair = shape(2, size, ch)
    ext = shape(size + edge, ch)
    e6 = shape(6 * cols, ch)

    def pack_edges(*groups):
        def spec(index, n, last):
            start = (rows - n) * cols if last else 0
            return pl.BlockSpec((pl.Element(1), pl.Element(n * cols), pl.Element(ch)), lambda i: (index, start, 0))

        parts = [(part, last) for group in groups for last in (True, False) for part in group]
        pixels = [sum(n for _, _, n in group) * cols for group in groups for _ in range(2)]
        return pl.pallas_call(
            functools.partial(pack, [len(group) for group in groups]), grid=(1,),
            out_shape=[shape(n, ch) for n in pixels],
            in_specs=[SMEM] + [spec(index, n, last) for (_, index, n), last in parts],
            out_specs=[pl.BlockSpec((n, ch), lambda i: (0, 0)) for n in pixels],
            compiler_params=pltpu.CompilerParams(vmem_limit_bytes=60 << 20), cost_estimate=LITTLE, name="pack_edges",
        )(at, *[array for (array, _, _), _ in parts])

    inner, outer, fwd_inner, fwd_outer = pack_edges(
        [(y, 0, 2), (g, 1, 2), (y, 1, 1), (g, 0, 1), (fresh, 1, 2), (fresh, 0, 1)], [(state, 1, 4), (state, 0, 3)]
    )
    edges0, fwd_edges = (swap(inner, outer), swap(fwd_inner, fwd_outer))
    (w_t,) = kernel(flip, at, (w,), (shape(2, 9 * ch, ch),))

    def extended(start, n, middle, edges, inset=0):
        (inner, outer), n = (edges, n * cols)
        above, below = ((start + inset) * cols, start * cols)
        yes, no = ((even_band, True), (even_band, False))
        return [
            (outer, None, above, n, yes), (inner, None, above, n, no), *middle,
            (inner, None, below, n, yes), (outer, None, below, n, no),
        ]

    def all_of(array, index):
        return [(array, index, 0, size, None)]

    mid = shape(2 * size - 6 * cols, ch)
    q2, h1, edges, mid_y, mid_g = kernel(
        functools.partial(invert, cols), at,
        (
            extended(0, 2, all_of(y, 0), edges0), extended(2, 2, all_of(g, 1), edges0),
            extended(4, 1, all_of(y, 1), edges0), extended(5, 1, all_of(g, 0), edges0),
            w_f, w_g, (w_t, 0), (w_t, 1),
        ),
        (ext, ext, shape(12 * cols, ch), mid, mid), [x_scratch(2)],
    )
    came_edges = along(edges, back_route)
    adv, ahead_q, ahead_p, mid_y, mid_g, token = kernel(
        functools.partial(advance, cols, 2), at,
        (
            extended(0, 4, all_of(state, 1), fwd_edges), extended(4, 3, all_of(state, 0), fwd_edges), w_f, w_g,
            extended(6, 2, all_of(fresh, 1), edges0), extended(8, 1, all_of(fresh, 0), edges0), mid_y, mid_g,
        ),
        (pair, shape(size + 4 * cols, ch), ext, mid, mid), [x_scratch(4)], token=True,
    )
    q, p = (along(ahead_q, ahead_ring), along(ahead_p, ahead_ring))
    came_mids = (along(mid_y, back_route), along(mid_g, back_route))
    terms, token = kernel(
        functools.partial(weight_terms, cols), at,
        (
            extended(0, 1, all_of(y, 0), edges0, 1), (g, 1),
            q2, [(h1, None, cols, size, None)],
        ),
        (shape(2, 9 * ch, ch),), [x_scratch(1)], (token,), True,
    )

    spans = ((0, 2, adv, 0), (2, 2, loss, (0, 1)), (4, 1, adv, 1), (5, 1, loss, (0, 0)))
    half = 6 * cols
    last, others = ((last_section, True), (last_section, False))
    picks = [
        [
            (came_edges, None, first + start * cols, n * cols, others),
            (own, index, size - n * cols if first else 0, n * cols, last),
        ]
        for first in (half, 0)
        for start, n, own, index in spans
    ]
    edges1 = swap(*kernel(pick, at, picks, (e6, e6)))
    inner, outer = (size - 2 * edge, size - edge)

    def came_field(k):
        start, n, own, index = spans[k]
        mid = came_mids[k % 2]
        return extended(start, n, [
            (came_edges, None, start * cols, n * cols, others),
            (mid, None, 0, inner, others) if k < 2 else (mid, None, inner, outer, others),
            (came_edges, None, half + start * cols, n * cols, others), (own, index, 0, size, last),
        ], edges1)

    last_adv, ahead, token = kernel(
        functools.partial(advance, cols, 0), at, (q, p, w_f, w_g, (fresh, 3), (fresh, 2)),
        (pair, pair), [x_scratch(2)], (token,), True,
    )
    (w_t,) = kernel(flip, at, (w,), (shape(2, 9 * ch, ch),), after=(token,))
    back, fields = kernel(
        functools.partial(invert_last, cols), at,
        (*[came_field(k) for k in range(4)], w_f, w_g, (w_t, 0), (w_t, 1), (loss, 1)),
        (shape(4, size, ch), shape(4, size + edge, ch)), [x_scratch(2)],
    )
    came_back = along(back, back_ring)
    part = 9 * ch // bands
    chunks = (2, 8, part, ch)
    keep, send = kernel(
        functools.partial(weight_sums, cols), at,
        ((fields, 2), [(fields, 3, cols, size, None)], (fields, 0), [(fields, 1, cols, size, None)], terms),
        (shape(*chunks, dtype=F32), shape(*chunks)), [x_scratch(1), pltpu.VMEM((9 * ch, ch), F32)],
    )

    def on_x(piece, step):
        return lax.ppermute(
            piece, "band", [(i, (i & 8) | ((((i >> 1) & 3) + step) % 4) << 1 | (i & 1)) for i in range(bands)]
        )

    def over_bands(send, keep, ahead, at):
        came_ahead = along(ahead, ahead_ring)
        came = lax.ppermute(send, "band", [(i, i ^ 1) for i in range(bands)])
        quarter = shape(2, 2, part, ch)
        own, far, right, left = kernel(
            sum_cores, at, (keep, came), (shape(2, 2, part, ch, dtype=F32), quarter, quarter, quarter)
        )
        far, right, left = (on_x(far, 2), on_x(right, 1), on_x(left, 3))
        send, keep = kernel(
            sum_chips, at, (own, far, right, left), (shape(2, part, ch), shape(2, part, ch, dtype=F32))
        )
        came = lax.ppermute(send, "band", [(i, i ^ 8) for i in range(bands)])
        return keep + came.astype(F32), came_ahead

    weight_grad, came_ahead = lax.cond(
        seg < segments, over_bands, lambda send, keep, ahead, at: (jnp.zeros((2, part, ch), F32), ahead),
        send, keep, ahead, at,
    )

    *outputs, weight_grad = pl.pallas_call(
        place_outputs, out_shape=[pair] * 3 + [shape(2, part, ch, dtype=F32)], in_specs=[SMEM] + [VMEM] * 2 + [ANY, VMEM],
        out_specs=[ANY] * 4,
        scratch_shapes=[pltpu.VMEM((2, size, ch), BF16), pltpu.SemaphoreType.DMA((5,))], cost_estimate=LITTLE,
        compiler_params=pltpu.CompilerParams(vmem_limit_bytes=8 << 20), name="place_outputs",
    )(at, came_ahead, came_back, last_adv, weight_grad)
    return (*[out.reshape(full) for out in outputs], weight_grad[None])


def solution(mesh):
    return jax.shard_map(
        local,
        mesh=mesh,
        in_specs=(
            P("segment", None, "band", None, None),
            P("segment", None, "band", None, None),
            P("segment", None, "band", None, None),
            P("segment", None, None, None),
            P(None, None, "band", None, None),
            P(None, None, "band", None, None),
        ),
        out_specs=(
            P("segment", None, "band", None, None),
            P("segment", None, "band", None, None),
            P("segment", None, "band", None, None),
            P("segment", None, "band", None),
        ),
        check_vma=False,
    )
```

```python
import functools

import jax
import jax.numpy as jnp
from jax import lax
from jax.experimental import pallas as pl
from jax.experimental.pallas import tpu as pltpu
from jax.sharding import PartitionSpec as P

F32 = jnp.float32
BF16 = jnp.bfloat16
ANY = pl.BlockSpec(memory_space=pl.ANY)
VMEM = pl.BlockSpec(memory_space=pltpu.VMEM)
SMEM = pl.BlockSpec(memory_space=pltpu.SMEM)
LITTLE = pl.CostEstimate(flops=1000, bytes_accessed=1000, transcendentals=0)


def shape(*dims, dtype=BF16):
    return jax.ShapeDtypeStruct(dims, dtype)


def last_section(at_ref):
    return at_ref[0] == at_ref[2] - 1


class View:
    def __init__(self, pieces, at_ref):
        self.pieces, self.at_ref = (pieces, at_ref)

    @property
    def ref(self):
        return self.pieces[0][0]

    def value(self):
        groups = []
        for ref, when in self.pieces:
            if when is None or not groups or groups[-1][0] is None:
                groups.append((None, [ref[...]]) if when is None else (0, ([], [])))
            if when is not None:
                groups[-1][1][int(when)].append(ref[...])
        parts = []
        for kind, group in groups:
            if kind is None:
                parts += group
            else:
                rest, last = (jnp.concatenate(g, 0) if len(g) > 1 else g[0] for g in group)
                parts.append(jnp.where(last_section(self.at_ref), last, rest))
        return parts[0] if len(parts) == 1 else jnp.concatenate(parts, 0)


def kernel(body, at, args, outs, scratch=(), after=(), token=False, mib=16):
    arrays = []
    outs = [*outs, shape(8, 128, dtype=F32)] if token else outs

    def place(array):
        for i, a in enumerate(arrays):
            if a is array:
                return i
        arrays.append(array)
        return len(arrays) - 1

    plan = []
    for arg in args:
        if not isinstance(arg, list):
            arg = [(*(arg if isinstance(arg, tuple) else (arg, None)), None, None, None)]
        plan.append([(place(piece[0]), *piece[1:]) for piece in arg])

    def run(*refs):
        at_ref, refs = (refs[len(after)], refs[len(after) + 1 :])
        views = []
        for pieces in plan:
            taken = []
            for i, index, start, size, when in pieces:
                ref = refs[i] if index is None else refs[i].at[index]
                taken.append((ref if start is None else ref.at[pl.ds(start, size)], when))
            views.append(View(taken, at_ref))
        refs = refs[len(arrays) :]
        body(at_ref, views, refs[: len(outs) - token], refs[len(outs) :])
        if token:
            refs[len(outs) - 1][...] = jnp.zeros((8, 128), F32)

    return pl.pallas_call(
        run,
        out_shape=outs,
        in_specs=[VMEM] * len(after) + [SMEM] + [VMEM] * len(arrays),
        out_specs=[VMEM] * len(outs),
        scratch_shapes=list(scratch),
        compiler_params=pltpu.CompilerParams(vmem_limit_bytes=mib << 20),
        cost_estimate=LITTLE,
        name=getattr(body, "func", body).__name__,
    )(*after, at, *arrays)


def sigmoid(v):
    return 1.0 / (1.0 + jnp.exp(-v))


def act(v):
    v = v.astype(F32)
    return (v * sigmoid(v)).astype(BF16).astype(F32)


def slope(v):
    v = v.astype(F32)
    s = sigmoid(v)
    return s * (1.0 + v * (1.0 - s))


def stencil(x_ref, v, cols):
    n, ch = v.shape
    v = v.astype(F32)
    col = lax.rem(lax.broadcasted_iota(jnp.int32, (n, ch), 0), cols)
    x_ref[:n, :ch] = jnp.where(col == 0, 0.0, pltpu.roll(v, 1, 0)).astype(BF16)
    x_ref[:n, ch : 2 * ch] = v.astype(BF16)
    x_ref[:n, 2 * ch :] = jnp.where(col == cols - 1, 0.0, pltpu.roll(v, n - 1, 0)).astype(BF16)


def conv(x_ref, w_ref, cols, size):
    depth = x_ref.shape[1]
    total = None
    for a in range(3):
        term = jnp.dot(
            x_ref[a * cols : a * cols + size, :], w_ref[a * depth : (a + 1) * depth, :], preferred_element_type=F32
        )
        total = term if total is None else total + term
    return total


def correlate(x_ref, d, cols):
    size = d.shape[0]
    return [
        lax.dot_general(
            x_ref[a * cols : a * cols + size, :], d, (((0,), (0,)), ((), ())), preferred_element_type=F32
        )
        for a in range(3)
    ]


def inside_image(at_ref, values, margin):
    n = values.shape[0]
    pixel = lax.broadcasted_iota(jnp.int32, values.shape, 0)
    low = jnp.where(at_ref[1] == 0, margin, 0)
    high = jnp.where(at_ref[1] == at_ref[3] - 1, n - margin, n)
    return jnp.where((pixel >= low) & (pixel < high), values, jnp.zeros_like(values))


def flip(at_ref, args, outs, own):
    w_ref = args[0].ref
    ch = w_ref.shape[2]
    for k in (1, 0):
        for t in range(9):
            outs[0][k, (8 - t) * ch : (9 - t) * ch, :] = w_ref[k, t * ch : (t + 1) * ch, :].T


def pack(counts, *refs):
    outs = refs[-len(counts) :]
    refs = list(refs)
    for count, out in zip(counts, outs):
        end = 0
        for _ in range(count):
            ref = refs.pop(0)
            size = ref.shape[-2]
            out[end : end + size] = ref[...].reshape(size, ref.shape[-1])
            end += size


def pick(at_ref, args, outs, own):
    for k, out in enumerate(outs):
        end = 0
        for arg in args[k * len(args) // len(outs) : (k + 1) * len(args) // len(outs)]:
            value = arg.value()
            out[end : end + value.shape[0]] = value
            end += value.shape[0]


def invert_second(cols, x_ref, at_ref, y1, g2, y2, g1, w_g, t_g):
    wide = y1.shape[0] - 2 * cols
    stencil(x_ref, act(y1), cols)
    q2 = inside_image(at_ref, (y2.astype(F32) - conv(x_ref, w_g, cols, wide)).astype(BF16), cols)
    stencil(x_ref, g2, cols)
    back = conv(x_ref, t_g, cols, wide)
    h1 = (g1.astype(F32) + slope(y1[cols : cols + wide]) * back).astype(BF16)
    return q2, inside_image(at_ref, h1, cols)


def invert_first(cols, x_ref, y1, g2, q2, h1, w_f, t_f):
    size = y1.shape[0]
    stencil(x_ref, act(q2), cols)
    p2 = (y1.astype(F32) - conv(x_ref, w_f, cols, size)).astype(BF16)
    stencil(x_ref, h1, cols)
    back = conv(x_ref, t_f, cols, size)
    h2 = (g2.astype(F32) + slope(q2[cols : cols + size]) * back).astype(BF16)
    return p2, h2


def invert(cols, at_ref, args, outs, own):
    y1, g2, y2, g1 = (arg.value() for arg in args[:4])
    w_f, w_g, t_f, t_g = (arg.ref for arg in args[4:])
    edge = 2 * cols
    size = y1.shape[0] - 2 * edge
    q2, h1 = invert_second(cols, own[0], at_ref, y1, g2, y2, g1, w_g, t_g)
    outs[0][...] = q2
    outs[1][...] = h1
    there = slice(edge, edge + size)
    p2, h2 = invert_first(cols, own[0], y1[there], g2[there], q2, h1, w_f, t_f)
    here = slice(cols, cols + size)
    edges = outs[2]
    half = edges.shape[0] // 2
    inner = size - 2 * edge
    for k, (two, one) in enumerate(((p2, q2[here]), (h2, h1[here]))):
        at = k * edge
        edges[at : at + edge] = two[:edge]
        edges[half + at : half + at + edge] = two[size - edge :]
        at = 2 * edge + k * cols
        edges[at : at + cols] = one[:cols]
        edges[half + at : half + at + cols] = one[size - cols :]
        outs[3 + k][:inner] = two[edge : size - edge]
        outs[3 + k][inner:] = one[cols : size - cols]


def invert_last(cols, at_ref, args, outs, own):
    y1, g2, y2, g1 = (arg.value() for arg in args[:4])
    w_f, w_g, t_f, t_g, loss = (arg.ref for arg in args[4:])
    edge = 2 * cols
    size = y1.shape[0] - 2 * edge
    here = slice(cols, cols + size)
    there = slice(edge, edge + size)
    q2, h1 = invert_second(cols, own[0], at_ref, y1, g2, y2, g1, w_g, t_g)
    p2, h2 = invert_first(cols, own[0], y1[there], g2[there], q2, h1, w_f, t_f)
    send, fields = outs
    first = at_ref[0] == 0
    send[0] = p2
    send[1] = q2[here]
    send[2] = jnp.where(first, loss[0], h1[here])
    send[3] = jnp.where(first, loss[1], h2)
    inside = slice(cols, cols + size + edge)
    for k, field in enumerate((q2, h1, y1[inside], g2[inside])):
        fields[k] = field


def advance(cols, extra, at_ref, args, outs, own):
    q, p, w_f, w_g, new_q, new_p = args[:6]
    x_ref = own[0]
    q = q.value()
    edge = 2 * cols
    wide = q.shape[0] - edge
    size = wide - edge
    margin = extra * cols
    stencil(x_ref, act(q), cols)
    out1 = (p.value().astype(F32) + conv(x_ref, w_f.ref, cols, wide)).astype(BF16)
    out1 = inside_image(at_ref, out1, margin + cols)
    stencil(x_ref, act(out1), cols)
    out2 = (q[edge : edge + size].astype(F32) + conv(x_ref, w_g.ref, cols, size)).astype(BF16)
    adv, send = outs[:2]
    here = size - 2 * margin
    adv[0] = out1[cols + margin : cols + margin + here]
    adv[1] = out2[margin : margin + here]
    last = last_section(at_ref)
    if extra:
        out2 = inside_image(at_ref, out2, margin)
        send[...] = jnp.where(last, new_q.value(), out2)
        outs[2][...] = jnp.where(last, new_p.value(), out1[margin : margin + here + edge])
        outs[3][...] = args[6].ref[...]
        outs[4][...] = args[7].ref[...]
    else:
        send[0] = jnp.where(last, new_p.value(), adv[0])
        send[1] = jnp.where(last, new_q.value(), out2)


def weight_terms(cols, at_ref, args, outs, own):
    x_ref = own[0]
    depth = x_ref.shape[1]
    for k, (v, d) in enumerate((args[2:4], args[0:2])):
        stencil(x_ref, act(v.value()), cols)
        for a, term in enumerate(correlate(x_ref, d.value(), cols)):
            outs[0][k, a * depth : (a + 1) * depth] = term.astype(BF16)


def weight_sums(cols, at_ref, args, outs, own):
    x_ref, total = own
    depth = x_ref.shape[1]
    even = lax.rem(at_ref[1], 2) == 0
    keep, send = outs
    rows = send.shape[2]
    before = args[4].ref
    for k, (v, d) in enumerate((args[2:4], args[0:2])):
        stencil(x_ref, act(v.value()), cols)
        for a, term in enumerate(correlate(x_ref, d.value(), cols)):
            part = slice(a * depth, (a + 1) * depth)
            total[part] = term + before[k, part].astype(F32)
        for j in range(send.shape[1]):
            one = total[2 * j * rows : (2 * j + 1) * rows]
            two = total[(2 * j + 1) * rows : (2 * j + 2) * rows]
            keep[k, j] = jnp.where(even, one, two)
            send[k, j] = jnp.where(even, two, one).astype(BF16)


def sum_cores(at_ref, args, outs, own):
    keep, came = (arg.ref for arg in args)
    x = lax.rem(at_ref[1] // 2, 4)
    for d, out in zip((0, 2, 1, 3), outs):
        to = lax.rem(x + d, 4)
        for k in range(2):
            for z in range(2):
                out[k, z] = (keep[k, 4 * z + to] + came[k, 4 * z + to].astype(F32)).astype(out.dtype)


def sum_chips(at_ref, args, outs, own):
    z = at_ref[1] // 8
    parts = [arg.ref for arg in args]
    for k in range(2):
        for out, at in ((outs[0], 1 - z), (outs[1], z)):
            value = parts[0][k, at]
            for part in parts[1:]:
                value = value + part[k, at].astype(F32)
            out[k] = value.astype(out.dtype)


def place_outputs(at_ref, ahead_ref, back_ref, adv_ref, grad_ref,
                  forward_ref, returning_ref, backward_ref, weight_ref, held, sem):
    last = last_section(at_ref)
    copies = [
        pltpu.make_async_copy(ahead_ref, forward_ref, sem.at[0]),
        pltpu.make_async_copy(back_ref.at[pl.ds(2, 2)], backward_ref, sem.at[1]),
        pltpu.make_async_copy(grad_ref, weight_ref, sem.at[3]),
    ]
    came = pltpu.make_async_copy(back_ref.at[pl.ds(0, 2)], returning_ref, sem.at[2])
    for copy in copies:
        copy.start()
    pl.when(jnp.logical_not(last))(came.start)

    @pl.when(last)
    def own():
        fetch = pltpu.make_async_copy(adv_ref, held, sem.at[4])
        fetch.start()
        fetch.wait()
        pltpu.make_async_copy(held, returning_ref, sem.at[2]).start()

    for copy in copies:
        copy.wait()
    came.wait()


def local(forward_state, returning_state, returning_grad, weights, fresh_input, loss_grad):
    full = forward_state.shape
    rows, cols, ch = full[2:]
    size = rows * cols
    edge = 2 * cols
    segments = lax.axis_size("segment")
    bands = lax.axis_size("band")
    seg = lax.axis_index("segment")
    at = jnp.stack([seg, lax.axis_index("band"), segments, bands]).astype(jnp.int32)

    def up_down(bottom, top):
        return (
            lax.ppermute(bottom, "band", [(i, i + 1) for i in range(bands - 1)]),
            lax.ppermute(top, "band", [(i + 1, i) for i in range(bands - 1)]),
        )

    back_route = [(i + 1, i) for i in range(segments - 1)]
    back_ring = [(i, (i - 1) % segments) for i in range(segments)]
    ahead_ring = [(i, (i + 1) % segments) for i in range(segments)]

    def along(block, route):
        return lax.ppermute(block, "segment", route)

    state = forward_state.reshape(2, size, ch)
    y = returning_state.reshape(2, size, ch)
    g = returning_grad.reshape(2, size, ch)
    fresh = fresh_input.reshape(4, size, ch)
    loss = loss_grad.reshape(2, 2, size, ch)
    w = weights[0]
    w_f, w_g = ((w, 0), (w, 1))

    def x_scratch(extra):
        return pltpu.VMEM((size + 2 * extra * cols, 3 * ch), BF16)

    pair = shape(2, size, ch)
    ext = shape(size + edge, ch)
    e6 = shape(6 * cols, ch)

    def pack_edges(*groups):
        def spec(index, n, last):
            start = (rows - n) * cols if last else 0
            return pl.BlockSpec((pl.Element(1), pl.Element(n * cols), pl.Element(ch)), lambda i: (index, start, 0))

        parts = [(part, last) for group in groups for last in (True, False) for part in group]
        pixels = [sum(n for _, _, n in group) * cols for group in groups for _ in range(2)]
        return pl.pallas_call(
            functools.partial(pack, [len(group) for group in groups for _ in range(2)]), grid=(1,),
            out_shape=[shape(n, ch) for n in pixels],
            in_specs=[spec(index, n, last) for (_, index, n), last in parts],
            out_specs=[pl.BlockSpec((n, ch), lambda i: (0, 0)) for n in pixels],
            compiler_params=pltpu.CompilerParams(vmem_limit_bytes=60 << 20), cost_estimate=LITTLE, name="pack_edges",
        )(*[array for (array, _, _), _ in parts])

    bottom, top, fwd_bottom, fwd_top = pack_edges(
        [(y, 0, 2), (g, 1, 2), (y, 1, 1), (g, 0, 1), (fresh, 1, 2), (fresh, 0, 1)], [(state, 1, 4), (state, 0, 3)]
    )
    up, down = up_down(bottom, top)
    fwd_up, fwd_down = up_down(fwd_bottom, fwd_top)
    (w_t,) = kernel(flip, at, (w,), (shape(2, 9 * ch, ch),))

    def extended(start, n, middle, up, down):
        start, n = (start * cols, n * cols)
        return [(up, None, start, n, None), *middle, (down, None, start, n, None)]

    def all_of(array, index):
        return [(array, index, 0, size, None)]

    mid = shape(2 * size - 6 * cols, ch)
    q2, h1, edges, mid_y, mid_g = kernel(
        functools.partial(invert, cols), at,
        (
            extended(0, 2, all_of(y, 0), up, down), extended(2, 2, all_of(g, 1), up, down),
            extended(4, 1, all_of(y, 1), up, down), extended(5, 1, all_of(g, 0), up, down),
            w_f, w_g, (w_t, 0), (w_t, 1),
        ),
        (ext, ext, shape(12 * cols, ch), mid, mid), [x_scratch(2)],
    )
    came_edges = along(edges, back_route)
    adv, ahead_q, ahead_p, mid_y, mid_g, token = kernel(
        functools.partial(advance, cols, 2), at,
        (
            extended(0, 4, all_of(state, 1), fwd_up, fwd_down), extended(4, 3, all_of(state, 0), fwd_up, fwd_down), w_f, w_g,
            extended(6, 2, all_of(fresh, 1), up, down), extended(8, 1, all_of(fresh, 0), up, down), mid_y, mid_g,
        ),
        (pair, shape(size + 4 * cols, ch), ext, mid, mid), [x_scratch(4)], token=True,
    )
    q, p = (along(ahead_q, ahead_ring), along(ahead_p, ahead_ring))
    came_mids = (along(mid_y, back_route), along(mid_g, back_route))
    terms, token = kernel(
        functools.partial(weight_terms, cols), at,
        (
            [(up, None, cols, cols, None), (y, 0, 0, size, None), (down, None, 0, cols, None)], (g, 1),
            q2, [(h1, None, cols, size, None)],
        ),
        (shape(2, 9 * ch, ch),), [x_scratch(1)], (token,), True,
    )

    spans = ((0, 2, adv, 0), (2, 2, loss, (0, 1)), (4, 1, adv, 1), (5, 1, loss, (0, 0)))
    half = 6 * cols
    picks = [
        [
            (came_edges, None, first + start * cols, n * cols, False),
            (own, index, size - n * cols if first else 0, n * cols, True),
        ]
        for first in (half, 0)
        for start, n, own, index in spans
    ]
    bottom, top = kernel(pick, at, picks, (e6, e6))
    up, down = up_down(bottom, top)
    inner, outer = (size - 2 * edge, size - edge)

    def came_field(k):
        start, n, own, index = spans[k]
        mid = came_mids[k % 2]
        return extended(start, n, [
            (came_edges, None, start * cols, n * cols, False),
            (mid, None, 0, inner, False) if k < 2 else (mid, None, inner, outer, False),
            (came_edges, None, half + start * cols, n * cols, False), (own, index, 0, size, True),
        ], up, down)

    last_adv, ahead, token = kernel(
        functools.partial(advance, cols, 0), at, (q, p, w_f, w_g, (fresh, 3), (fresh, 2)),
        (pair, pair), [x_scratch(2)], (token,), True,
    )
    (w_t,) = kernel(flip, at, (w,), (shape(2, 9 * ch, ch),), after=(token,))
    back, fields = kernel(
        functools.partial(invert_last, cols), at,
        (*[came_field(k) for k in range(4)], w_f, w_g, (w_t, 0), (w_t, 1), (loss, 1)),
        (shape(4, size, ch), shape(4, size + edge, ch)), [x_scratch(2)],
    )
    came_back = along(back, back_ring)
    part = 9 * ch // bands
    chunks = (2, 8, part, ch)
    keep, send = kernel(
        functools.partial(weight_sums, cols), at,
        ((fields, 2), [(fields, 3, cols, size, None)], (fields, 0), [(fields, 1, cols, size, None)], terms),
        (shape(*chunks, dtype=F32), shape(*chunks)), [x_scratch(1), pltpu.VMEM((9 * ch, ch), F32)],
    )

    def on_x(piece, step):
        return lax.ppermute(
            piece, "band", [(i, (i & 8) | ((((i >> 1) & 3) + step) % 4) << 1 | (i & 1)) for i in range(bands)]
        )

    def over_bands(send, keep, ahead, at):
        came_ahead = along(ahead, ahead_ring)
        came = lax.ppermute(send, "band", [(i, i ^ 1) for i in range(bands)])
        quarter = shape(2, 2, part, ch)
        own, far, right, left = kernel(
            sum_cores, at, (keep, came), (shape(2, 2, part, ch, dtype=F32), quarter, quarter, quarter)
        )
        far, right, left = (on_x(far, 2), on_x(right, 1), on_x(left, 3))
        send, keep = kernel(
            sum_chips, at, (own, far, right, left), (shape(2, part, ch), shape(2, part, ch, dtype=F32))
        )
        came = lax.ppermute(send, "band", [(i, i ^ 8) for i in range(bands)])
        return keep + came.astype(F32), came_ahead

    weight_grad, came_ahead = lax.cond(
        seg < segments, over_bands, lambda send, keep, ahead, at: (jnp.zeros((2, part, ch), F32), ahead),
        send, keep, ahead, at,
    )

    *outputs, weight_grad = pl.pallas_call(
        place_outputs, out_shape=[pair] * 3 + [shape(2, part, ch, dtype=F32)], in_specs=[SMEM] + [VMEM] * 2 + [ANY, VMEM],
        out_specs=[ANY] * 4,
        scratch_shapes=[pltpu.VMEM((2, size, ch), BF16), pltpu.SemaphoreType.DMA((5,))], cost_estimate=LITTLE,
        compiler_params=pltpu.CompilerParams(vmem_limit_bytes=8 << 20), name="place_outputs",
    )(at, came_ahead, came_back, last_adv, weight_grad)
    return (*[out.reshape(full) for out in outputs], weight_grad[None])


def solution(mesh):
    return jax.shard_map(
        local,
        mesh=mesh,
        in_specs=(
            P("segment", None, "band", None, None),
            P("segment", None, "band", None, None),
            P("segment", None, "band", None, None),
            P("segment", None, None, None),
            P(None, None, "band", None, None),
            P(None, None, "band", None, None),
        ),
        out_specs=(
            P("segment", None, "band", None, None),
            P("segment", None, "band", None, None),
            P("segment", None, "band", None, None),
            P("segment", None, "band", None),
        ),
        check_vma=False,
    )
```

```python
import functools

import jax
import jax.numpy as jnp
from jax import lax
from jax.experimental import pallas as pl
from jax.experimental.pallas import tpu as pltpu
from jax.sharding import PartitionSpec as P

F32 = jnp.float32
BF16 = jnp.bfloat16
ANY = pl.BlockSpec(memory_space=pl.ANY)
VMEM = pl.BlockSpec(memory_space=pltpu.VMEM)
SMEM = pl.BlockSpec(memory_space=pltpu.SMEM)
LITTLE = pl.CostEstimate(flops=1000, bytes_accessed=1000, transcendentals=0)


def shape(*dims, dtype=BF16):
    return jax.ShapeDtypeStruct(dims, dtype)


def last_section(at_ref):
    return at_ref[0] == at_ref[2] - 1


def even_band(at_ref):
    return lax.rem(at_ref[1], 2) == 0


class View:
    def __init__(self, pieces, at_ref):
        self.pieces, self.at_ref = (pieces, at_ref)

    @property
    def ref(self):
        return self.pieces[0][0]

    def value(self):
        groups = []
        for ref, when in self.pieces:
            test, truth = when if when else (None, False)
            if not groups or groups[-1][0] is not test:
                groups.append((test, ([], [])))
            groups[-1][1][truth].append(ref[...])
        parts = []
        for test, group in groups:
            no, yes = (jnp.concatenate(g, 0) if len(g) > 1 else g[0] if g else None for g in group)
            parts.append(no if test is None else jnp.where(test(self.at_ref), yes, no))
        return parts[0] if len(parts) == 1 else jnp.concatenate(parts, 0)


def kernel(body, at, args, outs, scratch=(), after=(), token=False, mib=16):
    arrays = []
    outs = [*outs, shape(8, 128, dtype=F32)] if token else outs

    def place(array):
        for i, a in enumerate(arrays):
            if a is array:
                return i
        arrays.append(array)
        return len(arrays) - 1

    plan = []
    for arg in args:
        if not isinstance(arg, list):
            arg = [(*(arg if isinstance(arg, tuple) else (arg, None)), None, None, None)]
        plan.append([(place(piece[0]), *piece[1:]) for piece in arg])

    def run(*refs):
        at_ref, refs = (refs[len(after)], refs[len(after) + 1 :])
        views = []
        for pieces in plan:
            taken = []
            for i, index, start, size, when in pieces:
                ref = refs[i] if index is None else refs[i].at[index]
                taken.append((ref if start is None else ref.at[pl.ds(start, size)], when))
            views.append(View(taken, at_ref))
        refs = refs[len(arrays) :]
        body(at_ref, views, refs[: len(outs) - token], refs[len(outs) :])
        if token:
            refs[len(outs) - 1][...] = jnp.zeros((8, 128), F32)

    return pl.pallas_call(
        run,
        out_shape=outs,
        in_specs=[VMEM] * len(after) + [SMEM] + [VMEM] * len(arrays),
        out_specs=[VMEM] * len(outs),
        scratch_shapes=list(scratch),
        compiler_params=pltpu.CompilerParams(vmem_limit_bytes=mib << 20),
        cost_estimate=LITTLE,
        name=getattr(body, "func", body).__name__,
    )(*after, at, *arrays)


def sigmoid(v):
    return 1.0 / (1.0 + jnp.exp(-v))


def act(v):
    v = v.astype(F32)
    return (v * sigmoid(v)).astype(BF16).astype(F32)


def slope(v):
    v = v.astype(F32)
    s = sigmoid(v)
    return s * (1.0 + v * (1.0 - s))


def stencil(x_ref, v, cols):
    n, ch = v.shape
    v = v.astype(F32)
    col = lax.rem(lax.broadcasted_iota(jnp.int32, (n, ch), 0), cols)
    x_ref[:n, :ch] = jnp.where(col == 0, 0.0, pltpu.roll(v, 1, 0)).astype(BF16)
    x_ref[:n, ch : 2 * ch] = v.astype(BF16)
    x_ref[:n, 2 * ch :] = jnp.where(col == cols - 1, 0.0, pltpu.roll(v, n - 1, 0)).astype(BF16)


def conv(x_ref, w_ref, cols, size):
    depth = x_ref.shape[1]
    total = None
    for a in range(3):
        term = jnp.dot(
            x_ref[a * cols : a * cols + size, :], w_ref[a * depth : (a + 1) * depth, :], preferred_element_type=F32
        )
        total = term if total is None else total + term
    return total


def correlate(x_ref, d, cols):
    size = d.shape[0]
    return [
        lax.dot_general(
            x_ref[a * cols : a * cols + size, :], d, (((0,), (0,)), ((), ())), preferred_element_type=F32
        )
        for a in range(3)
    ]


def inside_image(at_ref, values, margin):
    n = values.shape[0]
    pixel = lax.broadcasted_iota(jnp.int32, values.shape, 0)
    low = jnp.where(at_ref[1] == 0, margin, 0)
    high = jnp.where(at_ref[1] == at_ref[3] - 1, n - margin, n)
    return jnp.where((pixel >= low) & (pixel < high), values, jnp.zeros_like(values))


def flip(at_ref, args, outs, own):
    w_ref = args[0].ref
    ch = w_ref.shape[2]
    for k in (1, 0):
        for t in range(9):
            outs[0][k, (8 - t) * ch : (9 - t) * ch, :] = w_ref[k, t * ch : (t + 1) * ch, :].T


def by_band(at_ref, bottom, top, inner_ref, outer_ref):
    even = even_band(at_ref)
    inner_ref[...] = jnp.where(even, bottom, top)
    outer_ref[...] = jnp.where(even, top, bottom)


def pack(counts, at_ref, *refs):
    refs, outs = (list(refs), refs[-2 * len(counts) :])
    for k, count in enumerate(counts):
        sides = []
        for _ in range(2):
            sides.append(jnp.concatenate([refs.pop(0)[0] for _ in range(count)], 0))
        by_band(at_ref, *sides, *outs[2 * k : 2 * k + 2])


def pick(at_ref, args, outs, own):
    half = len(args) // 2
    sides = [jnp.concatenate([arg.value() for arg in part], 0) for part in (args[:half], args[half:])]
    by_band(at_ref, *sides, *outs)


def invert_second(cols, x_ref, at_ref, y1, g2, y2, g1, w_g, t_g):
    wide = y1.shape[0] - 2 * cols
    stencil(x_ref, act(y1), cols)
    q2 = inside_image(at_ref, (y2.astype(F32) - conv(x_ref, w_g, cols, wide)).astype(BF16), cols)
    stencil(x_ref, g2, cols)
    back = conv(x_ref, t_g, cols, wide)
    h1 = (g1.astype(F32) + slope(y1[cols : cols + wide]) * back).astype(BF16)
    return q2, inside_image(at_ref, h1, cols)


def invert_first(cols, x_ref, y1, g2, q2, h1, w_f, t_f):
    size = y1.shape[0]
    stencil(x_ref, act(q2), cols)
    p2 = (y1.astype(F32) - conv(x_ref, w_f, cols, size)).astype(BF16)
    stencil(x_ref, h1, cols)
    back = conv(x_ref, t_f, cols, size)
    h2 = (g2.astype(F32) + slope(q2[cols : cols + size]) * back).astype(BF16)
    return p2, h2


def invert(cols, at_ref, args, outs, own):
    y1, g2, y2, g1 = (arg.value() for arg in args[:4])
    w_f, w_g, t_f, t_g = (arg.ref for arg in args[4:])
    edge = 2 * cols
    size = y1.shape[0] - 2 * edge
    q2, h1 = invert_second(cols, own[0], at_ref, y1, g2, y2, g1, w_g, t_g)
    outs[0][...] = q2
    outs[1][...] = h1
    there = slice(edge, edge + size)
    p2, h2 = invert_first(cols, own[0], y1[there], g2[there], q2, h1, w_f, t_f)
    here = slice(cols, cols + size)
    edges = outs[2]
    half = edges.shape[0] // 2
    inner = size - 2 * edge
    for k, (two, one) in enumerate(((p2, q2[here]), (h2, h1[here]))):
        at = k * edge
        edges[at : at + edge] = two[:edge]
        edges[half + at : half + at + edge] = two[size - edge :]
        at = 2 * edge + k * cols
        edges[at : at + cols] = one[:cols]
        edges[half + at : half + at + cols] = one[size - cols :]
        outs[3 + k][:inner] = two[edge : size - edge]
        outs[3 + k][inner:] = one[cols : size - cols]


def invert_last(cols, at_ref, args, outs, own):
    y1, g2, y2, g1 = (arg.value() for arg in args[:4])
    w_f, w_g, t_f, t_g, loss = (arg.ref for arg in args[4:])
    edge = 2 * cols
    size = y1.shape[0] - 2 * edge
    here = slice(cols, cols + size)
    there = slice(edge, edge + size)
    q2, h1 = invert_second(cols, own[0], at_ref, y1, g2, y2, g1, w_g, t_g)
    p2, h2 = invert_first(cols, own[0], y1[there], g2[there], q2, h1, w_f, t_f)
    send, fields = outs
    first = at_ref[0] == 0
    send[0] = p2
    send[1] = q2[here]
    send[2] = jnp.where(first, loss[0], h1[here])
    send[3] = jnp.where(first, loss[1], h2)
    inside = slice(cols, cols + size + edge)
    for k, field in enumerate((q2, h1, y1[inside], g2[inside])):
        fields[k] = field


def advance(cols, extra, at_ref, args, outs, own):
    q, p, w_f, w_g, new_q, new_p = args[:6]
    x_ref = own[0]
    q = q.value()
    edge = 2 * cols
    wide = q.shape[0] - edge
    size = wide - edge
    margin = extra * cols
    stencil(x_ref, act(q), cols)
    out1 = (p.value().astype(F32) + conv(x_ref, w_f.ref, cols, wide)).astype(BF16)
    out1 = inside_image(at_ref, out1, margin + cols)
    stencil(x_ref, act(out1), cols)
    out2 = (q[edge : edge + size].astype(F32) + conv(x_ref, w_g.ref, cols, size)).astype(BF16)
    adv, send = outs[:2]
    here = size - 2 * margin
    adv[0] = out1[cols + margin : cols + margin + here]
    adv[1] = out2[margin : margin + here]
    last = last_section(at_ref)
    if extra:
        out2 = inside_image(at_ref, out2, margin)
        send[...] = jnp.where(last, new_q.value(), out2)
        outs[2][...] = jnp.where(last, new_p.value(), out1[margin : margin + here + edge])
        outs[3][...] = args[6].ref[...]
        outs[4][...] = args[7].ref[...]
    else:
        send[0] = jnp.where(last, new_p.value(), adv[0])
        send[1] = jnp.where(last, new_q.value(), out2)


def weight_terms(cols, at_ref, args, outs, own):
    x_ref = own[0]
    depth = x_ref.shape[1]
    for k, (v, d) in enumerate((args[2:4], args[0:2])):
        stencil(x_ref, act(v.value()), cols)
        for a, term in enumerate(correlate(x_ref, d.value(), cols)):
            outs[0][k, a * depth : (a + 1) * depth] = term.astype(BF16)


def weight_sums(cols, at_ref, args, outs, own):
    x_ref, total = own
    depth = x_ref.shape[1]
    even = lax.rem(at_ref[1], 2) == 0
    keep, send = outs
    rows = send.shape[2]
    before = args[4].ref
    for k, (v, d) in enumerate((args[2:4], args[0:2])):
        stencil(x_ref, act(v.value()), cols)
        for a, term in enumerate(correlate(x_ref, d.value(), cols)):
            part = slice(a * depth, (a + 1) * depth)
            total[part] = term + before[k, part].astype(F32)
        for j in range(send.shape[1]):
            one = total[2 * j * rows : (2 * j + 1) * rows]
            two = total[(2 * j + 1) * rows : (2 * j + 2) * rows]
            keep[k, j] = jnp.where(even, one, two)
            send[k, j] = jnp.where(even, two, one).astype(BF16)


def sum_cores(at_ref, args, outs, own):
    keep, came = (arg.ref for arg in args)
    x = lax.rem(at_ref[1] // 2, 4)
    for d, out in zip((0, 2, 1, 3), outs):
        to = lax.rem(x + d, 4)
        for k in range(2):
            for z in range(2):
                out[k, z] = (keep[k, 4 * z + to] + came[k, 4 * z + to].astype(F32)).astype(out.dtype)


def sum_chips(at_ref, args, outs, own):
    z = at_ref[1] // 8
    parts = [arg.ref for arg in args]
    for k in range(2):
        for out, at in ((outs[0], 1 - z), (outs[1], z)):
            value = parts[0][k, at]
            for part in parts[1:]:
                value = value + part[k, at].astype(F32)
            out[k] = value.astype(out.dtype)


def place_forward(ahead_ref, forward_ref, sem):
    copy = pltpu.make_async_copy(ahead_ref, forward_ref, sem)
    copy.start()
    copy.wait()


def place_outputs(at_ref, back_ref, adv_ref, grad_ref, returning_ref, backward_ref, weight_ref, held, sem):
    last = last_section(at_ref)
    copies = [
        pltpu.make_async_copy(back_ref.at[pl.ds(2, 2)], backward_ref, sem.at[1]),
        pltpu.make_async_copy(grad_ref, weight_ref, sem.at[3]),
    ]
    came = pltpu.make_async_copy(back_ref.at[pl.ds(0, 2)], returning_ref, sem.at[2])
    for copy in copies:
        copy.start()
    pl.when(jnp.logical_not(last))(came.start)

    @pl.when(last)
    def own():
        fetch = pltpu.make_async_copy(adv_ref, held, sem.at[4])
        fetch.start()
        fetch.wait()
        pltpu.make_async_copy(held, returning_ref, sem.at[2]).start()

    for copy in copies:
        copy.wait()
    came.wait()


def local(forward_state, returning_state, returning_grad, weights, fresh_input, loss_grad):
    full = forward_state.shape
    rows, cols, ch = full[2:]
    size = rows * cols
    edge = 2 * cols
    segments = lax.axis_size("segment")
    bands = lax.axis_size("band")
    seg = lax.axis_index("segment")
    at = jnp.stack([seg, lax.axis_index("band"), segments, bands]).astype(jnp.int32)

    def swap(inner, outer):
        return (
            lax.ppermute(inner, "band", [(i, i ^ 1) for i in range(bands)]),
            lax.ppermute(outer, "band", [(i, i + 1 if i % 2 else i - 1) for i in range(1, bands - 1)]),
        )

    back_route = [(i + 1, i) for i in range(segments - 1)]
    back_ring = [(i, (i - 1) % segments) for i in range(segments)]
    ahead_ring = [(i, (i + 1) % segments) for i in range(segments)]

    def along(block, route):
        return lax.ppermute(block, "segment", route)

    state = forward_state.reshape(2, size, ch)
    y = returning_state.reshape(2, size, ch)
    g = returning_grad.reshape(2, size, ch)
    fresh = fresh_input.reshape(4, size, ch)
    loss = loss_grad.reshape(2, 2, size, ch)
    w = weights[0]
    w_f, w_g = ((w, 0), (w, 1))

    def x_scratch(extra):
        return pltpu.VMEM((size + 2 * extra * cols, 3 * ch), BF16)

    pair = shape(2, size, ch)
    ext = shape(size + edge, ch)
    e6 = shape(6 * cols, ch)

    def pack_edges(*groups):
        def spec(index, n, last):
            start = (rows - n) * cols if last else 0
            return pl.BlockSpec((pl.Element(1), pl.Element(n * cols), pl.Element(ch)), lambda i: (index, start, 0))

        parts = [(part, last) for group in groups for last in (True, False) for part in group]
        pixels = [sum(n for _, _, n in group) * cols for group in groups for _ in range(2)]
        return pl.pallas_call(
            functools.partial(pack, [len(group) for group in groups]), grid=(1,),
            out_shape=[shape(n, ch) for n in pixels],
            in_specs=[SMEM] + [spec(index, n, last) for (_, index, n), last in parts],
            out_specs=[pl.BlockSpec((n, ch), lambda i: (0, 0)) for n in pixels],
            compiler_params=pltpu.CompilerParams(vmem_limit_bytes=60 << 20), cost_estimate=LITTLE, name="pack_edges",
        )(at, *[array for (array, _, _), _ in parts])

    inner, outer, fwd_inner, fwd_outer = pack_edges(
        [(y, 0, 2), (g, 1, 2), (y, 1, 1), (g, 0, 1), (fresh, 1, 2), (fresh, 0, 1)], [(state, 1, 4), (state, 0, 3)]
    )
    edges0, fwd_edges = (swap(inner, outer), swap(fwd_inner, fwd_outer))
    (w_t,) = kernel(flip, at, (w,), (shape(2, 9 * ch, ch),))

    def extended(start, n, middle, edges, inset=0):
        (inner, outer), n = (edges, n * cols)
        above, below = ((start + inset) * cols, start * cols)
        yes, no = ((even_band, True), (even_band, False))
        return [
            (outer, None, above, n, yes), (inner, None, above, n, no), *middle,
            (inner, None, below, n, yes), (outer, None, below, n, no),
        ]

    def all_of(array, index):
        return [(array, index, 0, size, None)]

    mid = shape(2 * size - 6 * cols, ch)
    q2, h1, edges, mid_y, mid_g = kernel(
        functools.partial(invert, cols), at,
        (
            extended(0, 2, all_of(y, 0), edges0), extended(2, 2, all_of(g, 1), edges0),
            extended(4, 1, all_of(y, 1), edges0), extended(5, 1, all_of(g, 0), edges0),
            w_f, w_g, (w_t, 0), (w_t, 1),
        ),
        (ext, ext, shape(12 * cols, ch), mid, mid), [x_scratch(2)],
    )
    came_edges = along(edges, back_route)
    adv, ahead_q, ahead_p, mid_y, mid_g, token = kernel(
        functools.partial(advance, cols, 2), at,
        (
            extended(0, 4, all_of(state, 1), fwd_edges), extended(4, 3, all_of(state, 0), fwd_edges), w_f, w_g,
            extended(6, 2, all_of(fresh, 1), edges0), extended(8, 1, all_of(fresh, 0), edges0), mid_y, mid_g,
        ),
        (pair, shape(size + 4 * cols, ch), ext, mid, mid), [x_scratch(4)], token=True,
    )
    q, p = (along(ahead_q, ahead_ring), along(ahead_p, ahead_ring))
    came_mids = (along(mid_y, back_route), along(mid_g, back_route))
    terms, token = kernel(
        functools.partial(weight_terms, cols), at,
        (
            extended(0, 1, all_of(y, 0), edges0, 1), (g, 1),
            q2, [(h1, None, cols, size, None)],
        ),
        (shape(2, 9 * ch, ch),), [x_scratch(1)], (token,), True,
    )

    spans = ((0, 2, adv, 0), (2, 2, loss, (0, 1)), (4, 1, adv, 1), (5, 1, loss, (0, 0)))
    half = 6 * cols
    last, others = ((last_section, True), (last_section, False))
    picks = [
        [
            (came_edges, None, first + start * cols, n * cols, others),
            (own, index, size - n * cols if first else 0, n * cols, last),
        ]
        for first in (half, 0)
        for start, n, own, index in spans
    ]
    edges1 = swap(*kernel(pick, at, picks, (e6, e6)))
    inner, outer = (size - 2 * edge, size - edge)

    def came_field(k):
        start, n, own, index = spans[k]
        mid = came_mids[k % 2]
        return extended(start, n, [
            (came_edges, None, start * cols, n * cols, others),
            (mid, None, 0, inner, others) if k < 2 else (mid, None, inner, outer, others),
            (came_edges, None, half + start * cols, n * cols, others), (own, index, 0, size, last),
        ], edges1)

    last_adv, ahead, token = kernel(
        functools.partial(advance, cols, 0), at, (q, p, w_f, w_g, (fresh, 3), (fresh, 2)),
        (pair, pair), [x_scratch(2)], (token,), True,
    )
    (w_t,) = kernel(flip, at, (w,), (shape(2, 9 * ch, ch),), after=(token,))
    back, fields = kernel(
        functools.partial(invert_last, cols), at,
        (*[came_field(k) for k in range(4)], w_f, w_g, (w_t, 0), (w_t, 1), (loss, 1)),
        (shape(4, size, ch), shape(4, size + edge, ch)), [x_scratch(2)],
    )
    came_back = along(back, back_ring)
    part = 9 * ch // bands
    chunks = (2, 8, part, ch)
    keep, send = kernel(
        functools.partial(weight_sums, cols), at,
        ((fields, 2), [(fields, 3, cols, size, None)], (fields, 0), [(fields, 1, cols, size, None)], terms),
        (shape(*chunks, dtype=F32), shape(*chunks)), [x_scratch(1), pltpu.VMEM((9 * ch, ch), F32)],
    )

    def on_x(piece, step):
        return lax.ppermute(
            piece, "band", [(i, (i & 8) | ((((i >> 1) & 3) + step) % 4) << 1 | (i & 1)) for i in range(bands)]
        )

    def over_bands(send, keep, ahead, at):
        came_ahead = along(ahead, ahead_ring)
        came = lax.ppermute(send, "band", [(i, i ^ 1) for i in range(bands)])
        quarter = shape(2, 2, part, ch)
        own, far, right, left = kernel(
            sum_cores, at, (keep, came), (shape(2, 2, part, ch, dtype=F32), quarter, quarter, quarter)
        )
        far, right, left = (on_x(far, 2), on_x(right, 1), on_x(left, 3))
        send, keep = kernel(
            sum_chips, at, (own, far, right, left), (shape(2, part, ch), shape(2, part, ch, dtype=F32))
        )
        came = lax.ppermute(send, "band", [(i, i ^ 8) for i in range(bands)])
        forward = pl.pallas_call(
            place_forward, out_shape=pair, in_specs=[VMEM], out_specs=ANY, scratch_shapes=[pltpu.SemaphoreType.DMA],
            cost_estimate=LITTLE, name="place_forward",
        )(came_ahead)
        return keep + came.astype(F32), forward

    weight_grad, forward = lax.cond(
        seg < segments, over_bands, lambda send, keep, ahead, at: (jnp.zeros((2, part, ch), F32), ahead),
        send, keep, ahead, at,
    )

    returning, backward, weight_grad = pl.pallas_call(
        place_outputs, out_shape=[pair] * 2 + [shape(2, part, ch, dtype=F32)], in_specs=[SMEM, VMEM, ANY, VMEM],
        out_specs=[ANY] * 3,
        scratch_shapes=[pltpu.VMEM((2, size, ch), BF16), pltpu.SemaphoreType.DMA((5,))], cost_estimate=LITTLE,
        compiler_params=pltpu.CompilerParams(vmem_limit_bytes=8 << 20), name="place_outputs",
    )(at, came_back, last_adv, weight_grad)
    return (forward.reshape(full), returning.reshape(full), backward.reshape(full), weight_grad[None])


def solution(mesh):
    return jax.shard_map(
        local,
        mesh=mesh,
        in_specs=(
            P("segment", None, "band", None, None),
            P("segment", None, "band", None, None),
            P("segment", None, "band", None, None),
            P("segment", None, None, None),
            P(None, None, "band", None, None),
            P(None, None, "band", None, None),
        ),
        out_specs=(
            P("segment", None, "band", None, None),
            P("segment", None, "band", None, None),
            P("segment", None, "band", None, None),
            P("segment", None, "band", None),
        ),
        check_vma=False,
    )
```

```python
import functools

import jax
import jax.numpy as jnp
from jax import lax
from jax.experimental import pallas as pl
from jax.experimental.pallas import tpu as pltpu
from jax.sharding import PartitionSpec as P

F32 = jnp.float32
BF16 = jnp.bfloat16
ANY = pl.BlockSpec(memory_space=pl.ANY)
VMEM = pl.BlockSpec(memory_space=pltpu.VMEM)
SMEM = pl.BlockSpec(memory_space=pltpu.SMEM)
LITTLE = pl.CostEstimate(flops=1000, bytes_accessed=1000, transcendentals=0)


def shape(*dims, dtype=BF16):
    return jax.ShapeDtypeStruct(dims, dtype)


def last_section(at_ref):
    return at_ref[0] == at_ref[2] - 1


def even_band(at_ref):
    return lax.rem(at_ref[1], 2) == 0


class View:
    def __init__(self, pieces, at_ref):
        self.pieces, self.at_ref = (pieces, at_ref)

    @property
    def ref(self):
        return self.pieces[0][0]

    def value(self):
        groups = []
        for ref, when in self.pieces:
            test, truth = when if when else (None, False)
            if not groups or groups[-1][0] is not test:
                groups.append((test, ([], [])))
            groups[-1][1][truth].append(ref[...])
        parts = []
        for test, group in groups:
            no, yes = (jnp.concatenate(g, 0) if len(g) > 1 else g[0] if g else None for g in group)
            parts.append(no if test is None else jnp.where(test(self.at_ref), yes, no))
        return parts[0] if len(parts) == 1 else jnp.concatenate(parts, 0)


def kernel(body, at, args, outs, scratch=(), after=(), token=False, mib=16):
    arrays = []
    outs = [*outs, shape(8, 128, dtype=F32)] if token else outs

    def place(array):
        for i, a in enumerate(arrays):
            if a is array:
                return i
        arrays.append(array)
        return len(arrays) - 1

    plan = []
    for arg in args:
        if not isinstance(arg, list):
            arg = [(*(arg if isinstance(arg, tuple) else (arg, None)), None, None, None)]
        plan.append([(place(piece[0]), *piece[1:]) for piece in arg])

    def run(*refs):
        at_ref, refs = (refs[len(after)], refs[len(after) + 1 :])
        views = []
        for pieces in plan:
            taken = []
            for i, index, start, size, when in pieces:
                ref = refs[i] if index is None else refs[i].at[index]
                taken.append((ref if start is None else ref.at[pl.ds(start, size)], when))
            views.append(View(taken, at_ref))
        refs = refs[len(arrays) :]
        body(at_ref, views, refs[: len(outs) - token], refs[len(outs) :])
        if token:
            refs[len(outs) - 1][...] = jnp.zeros((8, 128), F32)

    return pl.pallas_call(
        run,
        out_shape=outs,
        in_specs=[VMEM] * len(after) + [SMEM] + [VMEM] * len(arrays),
        out_specs=[VMEM] * len(outs),
        scratch_shapes=list(scratch),
        compiler_params=pltpu.CompilerParams(vmem_limit_bytes=mib << 20),
        cost_estimate=LITTLE,
        name=getattr(body, "func", body).__name__,
    )(*after, at, *arrays)


def sigmoid(v):
    return 1.0 / (1.0 + jnp.exp(-v))


def act(v):
    v = v.astype(F32)
    return (v * sigmoid(v)).astype(BF16).astype(F32)


def slope(v):
    v = v.astype(F32)
    s = sigmoid(v)
    return s * (1.0 + v * (1.0 - s))


def stencil(x_ref, v, cols):
    n, ch = v.shape
    v = v.astype(F32)
    col = lax.rem(lax.broadcasted_iota(jnp.int32, (n, ch), 0), cols)
    x_ref[:n, :ch] = jnp.where(col == 0, 0.0, pltpu.roll(v, 1, 0)).astype(BF16)
    x_ref[:n, ch : 2 * ch] = v.astype(BF16)
    x_ref[:n, 2 * ch :] = jnp.where(col == cols - 1, 0.0, pltpu.roll(v, n - 1, 0)).astype(BF16)


def conv(x_ref, w_ref, cols, size):
    depth = x_ref.shape[1]
    total = None
    for a in range(3):
        term = jnp.dot(
            x_ref[a * cols : a * cols + size, :], w_ref[a * depth : (a + 1) * depth, :], preferred_element_type=F32
        )
        total = term if total is None else total + term
    return total


def correlate(x_ref, d, cols):
    size = d.shape[0]
    return [
        lax.dot_general(
            x_ref[a * cols : a * cols + size, :], d, (((0,), (0,)), ((), ())), preferred_element_type=F32
        )
        for a in range(3)
    ]


def inside_image(at_ref, values, margin):
    n = values.shape[0]
    pixel = lax.broadcasted_iota(jnp.int32, values.shape, 0)
    low = jnp.where(at_ref[1] == 0, margin, 0)
    high = jnp.where(at_ref[1] == at_ref[3] - 1, n - margin, n)
    return jnp.where((pixel >= low) & (pixel < high), values, jnp.zeros_like(values))


def flip(at_ref, args, outs, own):
    w_ref = args[0].ref
    ch = w_ref.shape[2]
    for k in (1, 0):
        for t in range(9):
            outs[0][k, (8 - t) * ch : (9 - t) * ch, :] = w_ref[k, t * ch : (t + 1) * ch, :].T


def by_band(at_ref, bottom, top, inner_ref, outer_ref):
    even = even_band(at_ref)
    inner_ref[...] = jnp.where(even, bottom, top)
    outer_ref[...] = jnp.where(even, top, bottom)


def pack(counts, at_ref, *refs):
    refs, outs = (list(refs), refs[-2 * len(counts) :])
    for k, count in enumerate(counts):
        sides = []
        for _ in range(2):
            sides.append(jnp.concatenate([refs.pop(0)[0] for _ in range(count)], 0))
        by_band(at_ref, *sides, *outs[2 * k : 2 * k + 2])


def hold(back_ref, ready_ref, out_ref):
    pass


def signal(at_ref, args, outs, own):
    outs[0][...] = jnp.zeros_like(outs[0])


def pick(at_ref, args, outs, own):
    half = len(args) // 2
    sides = [jnp.concatenate([arg.value() for arg in part], 0) for part in (args[:half], args[half:])]
    by_band(at_ref, *sides, *outs)


def invert_second(cols, x_ref, at_ref, y1, g2, y2, g1, w_g, t_g):
    wide = y1.shape[0] - 2 * cols
    stencil(x_ref, act(y1), cols)
    q2 = inside_image(at_ref, (y2.astype(F32) - conv(x_ref, w_g, cols, wide)).astype(BF16), cols)
    stencil(x_ref, g2, cols)
    back = conv(x_ref, t_g, cols, wide)
    h1 = (g1.astype(F32) + slope(y1[cols : cols + wide]) * back).astype(BF16)
    return q2, inside_image(at_ref, h1, cols)


def invert_first(cols, x_ref, y1, g2, q2, h1, w_f, t_f):
    size = y1.shape[0]
    stencil(x_ref, act(q2), cols)
    p2 = (y1.astype(F32) - conv(x_ref, w_f, cols, size)).astype(BF16)
    stencil(x_ref, h1, cols)
    back = conv(x_ref, t_f, cols, size)
    h2 = (g2.astype(F32) + slope(q2[cols : cols + size]) * back).astype(BF16)
    return p2, h2


def invert(cols, at_ref, args, outs, own):
    y1, g2, y2, g1 = (arg.value() for arg in args[:4])
    w_f, w_g, t_f, t_g = (arg.ref for arg in args[4:])
    edge = 2 * cols
    size = y1.shape[0] - 2 * edge
    q2, h1 = invert_second(cols, own[0], at_ref, y1, g2, y2, g1, w_g, t_g)
    outs[0][...] = q2
    outs[1][...] = h1
    there = slice(edge, edge + size)
    p2, h2 = invert_first(cols, own[0], y1[there], g2[there], q2, h1, w_f, t_f)
    here = slice(cols, cols + size)
    edges = outs[2]
    half = edges.shape[0] // 2
    inner = size - 2 * edge
    for k, (two, one) in enumerate(((p2, q2[here]), (h2, h1[here]))):
        at = k * edge
        edges[at : at + edge] = two[:edge]
        edges[half + at : half + at + edge] = two[size - edge :]
        at = 2 * edge + k * cols
        edges[at : at + cols] = one[:cols]
        edges[half + at : half + at + cols] = one[size - cols :]
        outs[3 + k][:inner] = two[edge : size - edge]
        outs[3 + k][inner:] = one[cols : size - cols]


def invert_last(cols, at_ref, args, outs, own):
    y1, g2, y2, g1 = (arg.value() for arg in args[:4])
    w_f, w_g, t_f, t_g, loss = (arg.ref for arg in args[4:])
    edge = 2 * cols
    size = y1.shape[0] - 2 * edge
    here = slice(cols, cols + size)
    there = slice(edge, edge + size)
    q2, h1 = invert_second(cols, own[0], at_ref, y1, g2, y2, g1, w_g, t_g)
    p2, h2 = invert_first(cols, own[0], y1[there], g2[there], q2, h1, w_f, t_f)
    send, fields = outs
    first = at_ref[0] == 0
    send[0] = p2
    send[1] = q2[here]
    send[2] = jnp.where(first, loss[0], h1[here])
    send[3] = jnp.where(first, loss[1], h2)
    inside = slice(cols, cols + size + edge)
    for k, field in enumerate((q2, h1, y1[inside], g2[inside])):
        fields[k] = field


def advance(cols, extra, at_ref, args, outs, own):
    q, p, w_f, w_g, new_q, new_p = args[:6]
    x_ref = own[0]
    q = q.value()
    edge = 2 * cols
    wide = q.shape[0] - edge
    size = wide - edge
    margin = extra * cols
    stencil(x_ref, act(q), cols)
    out1 = (p.value().astype(F32) + conv(x_ref, w_f.ref, cols, wide)).astype(BF16)
    out1 = inside_image(at_ref, out1, margin + cols)
    stencil(x_ref, act(out1), cols)
    out2 = (q[edge : edge + size].astype(F32) + conv(x_ref, w_g.ref, cols, size)).astype(BF16)
    adv, send = outs[:2]
    here = size - 2 * margin
    adv[0] = out1[cols + margin : cols + margin + here]
    adv[1] = out2[margin : margin + here]
    last = last_section(at_ref)
    if extra:
        out2 = inside_image(at_ref, out2, margin)
        send[...] = jnp.where(last, new_q.value(), out2)
        outs[2][...] = jnp.where(last, new_p.value(), out1[margin : margin + here + edge])
        outs[3][...] = args[6].ref[...]
        outs[4][...] = args[7].ref[...]
    else:
        send[0] = jnp.where(last, new_p.value(), adv[0])
        send[1] = jnp.where(last, new_q.value(), out2)


def weight_terms(cols, at_ref, args, outs, own):
    x_ref = own[0]
    depth = x_ref.shape[1]
    for k, (v, d) in enumerate((args[2:4], args[0:2])):
        stencil(x_ref, act(v.value()), cols)
        for a, term in enumerate(correlate(x_ref, d.value(), cols)):
            outs[0][k, a * depth : (a + 1) * depth] = term.astype(BF16)


def weight_sums(cols, at_ref, args, outs, own):
    x_ref, total = own
    depth = x_ref.shape[1]
    even = lax.rem(at_ref[1], 2) == 0
    keep, send = outs
    rows = send.shape[2]
    before = args[4].ref
    for k, (v, d) in enumerate((args[2:4], args[0:2])):
        stencil(x_ref, act(v.value()), cols)
        for a, term in enumerate(correlate(x_ref, d.value(), cols)):
            part = slice(a * depth, (a + 1) * depth)
            total[part] = term + before[k, part].astype(F32)
        for j in range(send.shape[1]):
            one = total[2 * j * rows : (2 * j + 1) * rows]
            two = total[(2 * j + 1) * rows : (2 * j + 2) * rows]
            keep[k, j] = jnp.where(even, one, two)
            send[k, j] = jnp.where(even, two, one).astype(BF16)


def sum_cores(at_ref, args, outs, own):
    keep, came = (arg.ref for arg in args)
    x = lax.rem(at_ref[1] // 2, 4)
    for d, out in zip((0, 2, 1, 3), outs):
        to = lax.rem(x + d, 4)
        for k in range(2):
            for z in range(2):
                out[k, z] = (keep[k, 4 * z + to] + came[k, 4 * z + to].astype(F32)).astype(out.dtype)


def sum_chips(at_ref, args, outs, own):
    z = at_ref[1] // 8
    parts = [arg.ref for arg in args]
    for k in range(2):
        for out, at in ((outs[0], 1 - z), (outs[1], z)):
            value = parts[0][k, at]
            for part in parts[1:]:
                value = value + part[k, at].astype(F32)
            out[k] = value.astype(out.dtype)


def place_forward(ahead_ref, forward_ref, sem):
    copy = pltpu.make_async_copy(ahead_ref, forward_ref, sem)
    copy.start()
    copy.wait()


def place_outputs(at_ref, back_ref, adv_ref, grad_ref, returning_ref, backward_ref, weight_ref, held, sem):
    last = last_section(at_ref)
    copies = [
        pltpu.make_async_copy(back_ref.at[pl.ds(2, 2)], backward_ref, sem.at[1]),
        pltpu.make_async_copy(grad_ref, weight_ref, sem.at[3]),
    ]
    came = pltpu.make_async_copy(back_ref.at[pl.ds(0, 2)], returning_ref, sem.at[2])
    for copy in copies:
        copy.start()
    pl.when(jnp.logical_not(last))(came.start)

    @pl.when(last)
    def own():
        fetch = pltpu.make_async_copy(adv_ref, held, sem.at[4])
        fetch.start()
        fetch.wait()
        pltpu.make_async_copy(held, returning_ref, sem.at[2]).start()

    for copy in copies:
        copy.wait()
    came.wait()


def local(forward_state, returning_state, returning_grad, weights, fresh_input, loss_grad):
    full = forward_state.shape
    rows, cols, ch = full[2:]
    size = rows * cols
    edge = 2 * cols
    segments = lax.axis_size("segment")
    bands = lax.axis_size("band")
    seg = lax.axis_index("segment")
    at = jnp.stack([seg, lax.axis_index("band"), segments, bands]).astype(jnp.int32)

    def swap(inner, outer):
        return (
            lax.ppermute(inner, "band", [(i, i ^ 1) for i in range(bands)]),
            lax.ppermute(outer, "band", [(i, i + 1 if i % 2 else i - 1) for i in range(1, bands - 1)]),
        )

    back_route = [(i + 1, i) for i in range(segments - 1)]
    back_ring = [(i, (i - 1) % segments) for i in range(segments)]
    ahead_ring = [(i, (i + 1) % segments) for i in range(segments)]

    def along(block, route):
        return lax.ppermute(block, "segment", route)

    state = forward_state.reshape(2, size, ch)
    y = returning_state.reshape(2, size, ch)
    g = returning_grad.reshape(2, size, ch)
    fresh = fresh_input.reshape(4, size, ch)
    loss = loss_grad.reshape(2, 2, size, ch)
    w = weights[0]
    w_f, w_g = ((w, 0), (w, 1))

    def x_scratch(extra):
        return pltpu.VMEM((size + 2 * extra * cols, 3 * ch), BF16)

    pair = shape(2, size, ch)
    ext = shape(size + edge, ch)
    e6 = shape(6 * cols, ch)

    def pack_edges(*groups):
        def spec(index, n, last):
            start = (rows - n) * cols if last else 0
            return pl.BlockSpec((pl.Element(1), pl.Element(n * cols), pl.Element(ch)), lambda i: (index, start, 0))

        parts = [(part, last) for group in groups for last in (True, False) for part in group]
        pixels = [sum(n for _, _, n in group) * cols for group in groups for _ in range(2)]
        return pl.pallas_call(
            functools.partial(pack, [len(group) for group in groups]), grid=(1,),
            out_shape=[shape(n, ch) for n in pixels],
            in_specs=[SMEM] + [spec(index, n, last) for (_, index, n), last in parts],
            out_specs=[pl.BlockSpec((n, ch), lambda i: (0, 0)) for n in pixels],
            compiler_params=pltpu.CompilerParams(vmem_limit_bytes=60 << 20), cost_estimate=LITTLE, name="pack_edges",
        )(at, *[array for (array, _, _), _ in parts])

    inner, outer, fwd_inner, fwd_outer = pack_edges(
        [(y, 0, 2), (g, 1, 2), (y, 1, 1), (g, 0, 1), (fresh, 1, 2), (fresh, 0, 1)], [(state, 1, 4), (state, 0, 3)]
    )
    edges0, fwd_edges = (swap(inner, outer), swap(fwd_inner, fwd_outer))
    (w_t,) = kernel(flip, at, (w,), (shape(2, 9 * ch, ch),))

    def extended(start, n, middle, edges, inset=0):
        (inner, outer), n = (edges, n * cols)
        above, below = ((start + inset) * cols, start * cols)
        yes, no = ((even_band, True), (even_band, False))
        return [
            (outer, None, above, n, yes), (inner, None, above, n, no), *middle,
            (inner, None, below, n, yes), (outer, None, below, n, no),
        ]

    def all_of(array, index):
        return [(array, index, 0, size, None)]

    mid = shape(2 * size - 6 * cols, ch)
    q2, h1, edges, mid_y, mid_g = kernel(
        functools.partial(invert, cols), at,
        (
            extended(0, 2, all_of(y, 0), edges0), extended(2, 2, all_of(g, 1), edges0),
            extended(4, 1, all_of(y, 1), edges0), extended(5, 1, all_of(g, 0), edges0),
            w_f, w_g, (w_t, 0), (w_t, 1),
        ),
        (ext, ext, shape(12 * cols, ch), mid, mid), [x_scratch(2)],
    )
    came_edges = along(edges, back_route)
    adv, ahead_q, ahead_p, mid_y, mid_g, token = kernel(
        functools.partial(advance, cols, 2), at,
        (
            extended(0, 4, all_of(state, 1), fwd_edges), extended(4, 3, all_of(state, 0), fwd_edges), w_f, w_g,
            extended(6, 2, all_of(fresh, 1), edges0), extended(8, 1, all_of(fresh, 0), edges0), mid_y, mid_g,
        ),
        (pair, shape(size + 4 * cols, ch), ext, mid, mid), [x_scratch(4)], token=True,
    )
    q, p = (along(ahead_q, ahead_ring), along(ahead_p, ahead_ring))
    came_mids = (along(mid_y, back_route), along(mid_g, back_route))
    terms, token = kernel(
        functools.partial(weight_terms, cols), at,
        (
            extended(0, 1, all_of(y, 0), edges0, 1), (g, 1),
            q2, [(h1, None, cols, size, None)],
        ),
        (shape(2, 9 * ch, ch),), [x_scratch(1)], (token,), True,
    )

    spans = ((0, 2, adv, 0), (2, 2, loss, (0, 1)), (4, 1, adv, 1), (5, 1, loss, (0, 0)))
    half = 6 * cols
    last, others = ((last_section, True), (last_section, False))
    picks = [
        [
            (came_edges, None, first + start * cols, n * cols, others),
            (own, index, size - n * cols if first else 0, n * cols, last),
        ]
        for first in (half, 0)
        for start, n, own, index in spans
    ]
    edges1 = swap(*kernel(pick, at, picks, (e6, e6)))
    inner, outer = (size - 2 * edge, size - edge)

    def came_field(k):
        start, n, own, index = spans[k]
        mid = came_mids[k % 2]
        return extended(start, n, [
            (came_edges, None, start * cols, n * cols, others),
            (mid, None, 0, inner, others) if k < 2 else (mid, None, inner, outer, others),
            (came_edges, None, half + start * cols, n * cols, others), (own, index, 0, size, last),
        ], edges1)

    last_adv, ahead, token = kernel(
        functools.partial(advance, cols, 0), at, (q, p, w_f, w_g, (fresh, 3), (fresh, 2)),
        (pair, pair), [x_scratch(2)], (token,), True,
    )
    w_t, token = kernel(flip, at, (w,), (shape(2, 9 * ch, ch),), after=(token,), token=True)
    back, fields = kernel(
        functools.partial(invert_last, cols), at,
        (*[came_field(k) for k in range(4)], w_f, w_g, (w_t, 0), (w_t, 1), (loss, 1)),
        (shape(4, size, ch), shape(4, size + edge, ch)), [x_scratch(2)],
    )
    (ready,) = kernel(signal, at, (), (shape(16, 128),), after=(*came_mids, token))
    ahead_on_z = [
        (16 * s + b, 16 * s + b + 8 if b < 8 else 16 * (s // 4 * 4 + (s + 1) % 4) + b - 8)
        for s in range(segments) for b in range(bands)
    ]
    ready = lax.ppermute(ready, ("segment", "band"), ahead_on_z)
    back = pl.pallas_call(
        hold, out_shape=shape(4, size, ch), in_specs=[ANY, VMEM], out_specs=ANY, input_output_aliases={0: 0},
        cost_estimate=LITTLE, name="hold",
    )(back, ready)
    came_back = along(back, back_ring)
    part = 9 * ch // bands
    chunks = (2, 8, part, ch)
    keep, send = kernel(
        functools.partial(weight_sums, cols), at,
        ((fields, 2), [(fields, 3, cols, size, None)], (fields, 0), [(fields, 1, cols, size, None)], terms),
        (shape(*chunks, dtype=F32), shape(*chunks)), [x_scratch(1), pltpu.VMEM((9 * ch, ch), F32)],
    )

    def on_x(piece, step):
        return lax.ppermute(
            piece, "band", [(i, (i & 8) | ((((i >> 1) & 3) + step) % 4) << 1 | (i & 1)) for i in range(bands)]
        )

    def over_bands(send, keep, ahead, at):
        came_ahead = along(ahead, ahead_ring)
        came = lax.ppermute(send, "band", [(i, i ^ 1) for i in range(bands)])
        quarter = shape(2, 2, part, ch)
        own, far, right, left = kernel(
            sum_cores, at, (keep, came), (shape(2, 2, part, ch, dtype=F32), quarter, quarter, quarter)
        )
        far, right, left = (on_x(far, 2), on_x(right, 1), on_x(left, 3))
        send, keep = kernel(
            sum_chips, at, (own, far, right, left), (shape(2, part, ch), shape(2, part, ch, dtype=F32))
        )
        came = lax.ppermute(send, "band", [(i, i ^ 8) for i in range(bands)])
        forward = pl.pallas_call(
            place_forward, out_shape=pair, in_specs=[VMEM], out_specs=ANY, scratch_shapes=[pltpu.SemaphoreType.DMA],
            cost_estimate=LITTLE, name="place_forward",
        )(came_ahead)
        return keep + came.astype(F32), forward

    weight_grad, forward = lax.cond(
        seg < segments, over_bands, lambda send, keep, ahead, at: (jnp.zeros((2, part, ch), F32), ahead),
        send, keep, ahead, at,
    )

    returning, backward, weight_grad = pl.pallas_call(
        place_outputs, out_shape=[pair] * 2 + [shape(2, part, ch, dtype=F32)], in_specs=[SMEM, VMEM, ANY, VMEM],
        out_specs=[ANY] * 3,
        scratch_shapes=[pltpu.VMEM((2, size, ch), BF16), pltpu.SemaphoreType.DMA((5,))], cost_estimate=LITTLE,
        compiler_params=pltpu.CompilerParams(vmem_limit_bytes=8 << 20), name="place_outputs",
    )(at, came_back, last_adv, weight_grad)
    return (forward.reshape(full), returning.reshape(full), backward.reshape(full), weight_grad[None])


def solution(mesh):
    return jax.shard_map(
        local,
        mesh=mesh,
        in_specs=(
            P("segment", None, "band", None, None),
            P("segment", None, "band", None, None),
            P("segment", None, "band", None, None),
            P("segment", None, None, None),
            P(None, None, "band", None, None),
            P(None, None, "band", None, None),
        ),
        out_specs=(
            P("segment", None, "band", None, None),
            P("segment", None, "band", None, None),
            P("segment", None, "band", None, None),
            P("segment", None, "band", None),
        ),
        check_vma=False,
    )
```
